128 devices in a mesh: mesh: 32 (over z, x, core), vec: 4 (over y).
Axes of the slice: x: 4, y: 4, z: 4, core: 2. Of those that a mesh axis runs over, the one named last changes fastest.
Arguments:
- panel: float32 [262144, 128], P('mesh', 'vec'), may hold values from -6 to 6
- orient: int32 [262144], P('mesh'), may hold values from -1 to 1, as said below
- mass: float32 [262144], P('mesh'), may hold values from 0.5 to 2
- stiff_diag: bfloat16 [2048, 128, 128], P('mesh'), may hold values from -0.05 to 4, as said below
- near_coupling: bfloat16 [2048, 128, 128], P('mesh'), may hold values from -0.1796875 to 0.1796875
- far_coupling: bfloat16 [2048, 128, 128], P('mesh'), may hold values from -0.1796875 to 0.1796875
Outputs:
- filtered: float32 [262144, 128], P('mesh', 'vec')
- ritz_stiff: float32 [128, 128], P('vec', 'mesh')
- ritz_mass: float32 [128, 128], P('vec', 'mesh')
The draws below stay inside these ranges and needn't reach their ends.
Inputs may be any that keep to these rules, and one draw needn't show every extreme that they name: `orient`: every entry is +1 or -1. `stiff_diag`: each block is symmetric; its diagonal entries lie from 2 to 4 and its off-diagonal entries have magnitude at most 0.05.
All inputs are finite; a program needn't handle non-finite values.
Results may differ from the reference program's by a relative error of at most 0.0035.
Values may be sent and summed in bfloat16 or wider, within the bound.
A program may use at most 64 MiB of HBM per device.

```python
import math
import jax
import jax.numpy as jnp
from jax import lax

BS = 128
VECS = 128
SPAN = 32
DEGREE = 4
APPS = 2
NBLK = 2048
EDGES = 262144


def draw_orient(key, part):
    return (2 * jax.random.randint(key, (NBLK * BS,), 0, 2) - 1).astype(jnp.int32)


def draw_stiff_diag(key, part):
    first, second = jax.random.split(key)
    noise = jnp.clip(0.03 * jax.random.normal(first, (NBLK, BS, BS), jnp.float32), -0.049, 0.049)
    symmetric = 0.5 * (noise + jnp.swapaxes(noise, 1, 2))
    diagonal = jax.random.uniform(second, (NBLK, BS, 1), jnp.float32, 2.0, 4.0)
    identity = jnp.eye(BS, dtype=jnp.float32)
    return (symmetric * (1.0 - identity) + identity * diagonal).astype(jnp.bfloat16)


def spiked(result, key, source, target, blocks, factor):
    owner, partner = [(jnp.arange(result.shape[axis_at]) // (result.shape[axis_at] // blocks)).reshape([-1 if axis == axis_at else 1 for axis in range(result.ndim)]) for axis_at in (source, target)]
    chosen = jax.random.permutation(key, blocks)[partner]
    strong = (owner == chosen) | (owner == (partner + blocks // 2) % blocks)
    return jnp.where(strong, factor * result, result)


def shard_levels(key, extent, shards, low, largest):
    level, own = 1.0, jax.random.fold_in(key, 6)
    for position, parts in shards:
        heights = jnp.exp(jax.random.uniform(jax.random.fold_in(own, position), (parts,), jnp.float32, low / len(shards), largest / len(shards)))
        level = level * jnp.repeat(heights, extent[position] // parts).reshape([-1 if axis == position else 1 for axis in range(len(extent))])
    return level


def gaussian(stream_key, dims, width, reach, shards=(), kind=jnp.bfloat16):
    entries = jax.random.normal(stream_key, dims, jnp.float32) * width
    if len(shards) > 0:
        entries = shard_levels(stream_key, dims, shards, -0.22, 0.18) * entries
    return jnp.clip(entries, min=-reach, max=reach).astype(kind)


def noise_with(own_key, extent, scale, reach, pieces, heavy, kind=jnp.bfloat16):
    entries = scale * jax.random.normal(own_key, extent, jnp.float32)
    if pieces:
        entries = entries * shard_levels(own_key, extent, pieces, -0.22, 0.18)
    return jnp.clip(spiked(entries, jax.random.fold_in(own_key, 3), *heavy), -reach, reach).astype(kind)


def setup_inputs(seed: int = 0) -> dict:
    seeds = jax.random.split(jax.random.key(seed), 7)
    panel = noise_with(seeds[0], (EDGES, VECS), 1.0, 6.0, ((0, 32), (1, 4)), (0, 1, 32, 2.75), jnp.float32)
    orient = draw_orient(jax.random.fold_in(seeds[6], 71), 0)
    mass = jnp.clip(jnp.exp(math.log(2.0) - 1.3862944 * jax.random.uniform(seeds[2], (EDGES,), jnp.float32) ** shard_levels(seeds[2], (EDGES,), ((0, 32),), -0.2, 0.2)), 0.5, 2.0)
    stiff_diag = draw_stiff_diag(jax.random.fold_in(seeds[6], 71), 0)
    near_coupling = gaussian(seeds[4], (NBLK, BS, BS), 0.03, 0.1796875, ((0, 32),))
    far_coupling = gaussian(seeds[5], (NBLK, BS, BS), 0.03, 0.1796875, ((0, 32),))
    return dict(panel=panel, orient=orient, mass=mass, stiff_diag=stiff_diag, near_coupling=near_coupling, far_coupling=far_coupling)


filter_center = 6.0
filter_radius = 8.0

def shift_down(values, amount):
    pad = jnp.zeros((amount,) + values.shape[1:], values.dtype)
    return jnp.concatenate([pad, values[:-amount]], axis=0)

def shift_up(values, amount):
    pad = jnp.zeros((amount,) + values.shape[1:], values.dtype)
    return jnp.concatenate([values[amount:], pad], axis=0)

def reference(panel, orient, mass, stiff_diag, near_coupling, far_coupling):
    highest = lax.Precision.HIGHEST
    scale = orient.astype(jnp.float32) / jnp.sqrt(mass)
    diag_full = stiff_diag.astype(jnp.float32)
    near_full = near_coupling.astype(jnp.float32)
    far_full = far_coupling.astype(jnp.float32)

    def operate(field):
        scaled = (scale[:, None] * field).astype(jnp.bfloat16).astype(jnp.float32)
        blocks = scaled.reshape(NBLK, BS, VECS)
        total = jnp.einsum('bij,bjc->bic', diag_full, blocks, precision=highest)
        total = total + jnp.einsum('bij,bjc->bic', near_full, shift_down(blocks, 1), precision=highest)
        total = total + shift_up(jnp.einsum('bji,bjc->bic', near_full, blocks, precision=highest), 1)
        total = total + jnp.einsum('bij,bjc->bic', far_full, shift_down(blocks, SPAN), precision=highest)
        total = total + shift_up(jnp.einsum('bji,bjc->bic', far_full, blocks, precision=highest), SPAN)
        return scale[:, None] * total.reshape(EDGES, VECS)

    def chebyshev(start):
        before = start
        current = (operate(start) - filter_center * start) / filter_radius
        for step in range(DEGREE - 1):
            following = 2.0 * (operate(current) - filter_center * current) / filter_radius - before
            before, current = (current, following)
        return current
    filtered = panel
    for application in range(APPS):
        filtered = chebyshev(filtered)
    image = operate(filtered)
    filtered_b = filtered.astype(jnp.bfloat16)
    image_b = image.astype(jnp.bfloat16)
    ritz_stiff = jnp.dot(filtered_b.T, image_b, preferred_element_type=jnp.float32)
    ritz_mass = jnp.dot(filtered_b.T, filtered_b, preferred_element_type=jnp.float32)
    return (filtered, ritz_stiff, ritz_mass)
```

```python
import functools

import jax
import jax.numpy as jnp
from jax import lax
from jax.experimental import pallas as pl
from jax.experimental.pallas import tpu as pltpu
from jax.sharding import PartitionSpec as P

SPAN = 32
BS = 128
DEGREE = 4
APPS = 2
NOPS = DEGREE * APPS
CENTER = 6.0

HALF = SPAN
STEPS = 4
CH = HALF // STEPS

MESH = pl.DeviceIdType.MESH
NT = (((1,), (1,)), ((), ()))
NN = (((1,), (0,)), ((), ()))
F32 = jnp.float32
BF16 = jnp.bfloat16


def block_of(q):
    return HALF * (q // HALF) + (q % HALF + 1) % HALF


def place_of(b):
    return HALF * (b // HALF) + (b % HALF - 1) % HALF


def lanes(q, n=1):
    return slice(q * BS, (q + n) * BS)


def dot(a, b, dims):
    return lax.dot_general(a, b, dims, preferred_element_type=F32)


def pieces():
    runs = []
    for s in range(STEPS):
        count = CH if s < STEPS - 1 else CH - 1
        runs.append((s * CH, s * CH + 1, count))
    runs.append((HALF - 1, 0, 1))
    return runs


RUNS = pieces()
NRUN = len(RUNS)


def runs_of(s):
    return (s,) if s < STEPS - 1 else (s, s + 1)


def kernel(
    nm, nv,
    x_hbm, orient_hbm, mass_hbm, diag_hbm, near_hbm, far_hbm,
    out_hbm, stiff_ref, massg_ref,
    orient, mass, scale, diag, near, far,
    x, acc, u, halo_u, p_out, halo_p,
    f_out, g_out, f_all, g_all, q_buf, t_buf, r_buf, s_buf, r2_buf,
    vec_sem, x_sem, far_sem, mat_sem, o_sem,
    us_sem, ur_sem, ps_sem, pr_sem,
    fs_sem, fr_sem, gs_sem, gr_sem,
    ts_sem, tr_sem, s2_sem, r2_sem,
):
    m = lax.axis_index("mesh")
    v = lax.axis_index("vec")

    cp_or = pltpu.make_async_copy(orient_hbm, orient, vec_sem.at[0])
    cp_ma = pltpu.make_async_copy(mass_hbm, mass, vec_sem.at[1])
    cp_or.start()
    cp_ma.start()

    def x_copy(h, r):
        pos, blk, n = RUNS[r]
        return pltpu.make_async_copy(
            x_hbm.at[:, lanes(h * HALF + blk, n)],
            x.at[0, :, lanes(h * HALF + pos, n)],
            x_sem.at[h, r],
        )

    def far_copy(r):
        _, blk, n = RUNS[r]
        return pltpu.make_async_copy(far_hbm.at[pl.ds(blk, n)], far.at[pl.ds(blk, n)], far_sem.at[r])

    for r in range(NRUN):
        x_copy(0, r).start()
        x_copy(1, r).start()
        far_copy(r).start()

    mats = [
        pltpu.make_async_copy(far_hbm.at[pl.ds(HALF, HALF)], far.at[pl.ds(HALF, HALF)], mat_sem.at[0]),
        pltpu.make_async_copy(diag_hbm, diag, mat_sem.at[1]),
        pltpu.make_async_copy(near_hbm, near, mat_sem.at[2]),
    ]
    for c in mats:
        c.start()

    @pl.when(m == 0)
    def _():
        halo_u[...] = jnp.zeros_like(halo_u)

    @pl.when(m == nm - 1)
    def _():
        halo_p[...] = jnp.zeros_like(halo_p)

    barrier = pltpu.get_barrier_semaphore()

    def hello_mesh(d, carry):
        pl.semaphore_signal(barrier, inc=1, device_id=(lax.rem(m + d, nm), v), device_id_type=MESH)
        return carry

    lax.fori_loop(1, nm, hello_mesh, 0)
    for d in range(1, nv):
        pl.semaphore_signal(barrier, inc=1, device_id=(m, lax.rem(v + d, nv)), device_id_type=MESH)

    cp_or.wait()
    cp_ma.wait()
    scale[...] = orient[...].astype(F32) / jnp.sqrt(mass[...])

    pl.semaphore_wait(barrier, nm - 1 + nv - 1)

    def send_u(par, s):
        return pltpu.make_async_remote_copy(
            src_ref=u.at[:, lanes(HALF + s * CH, CH)],
            dst_ref=halo_u.at[par, :, lanes(s * CH, CH)],
            send_sem=us_sem.at[s],
            recv_sem=ur_sem.at[par, s],
            device_id=(m + 1, v),
            device_id_type=MESH,
        )

    def send_p(par, s):
        n = CH + (s == STEPS - 1)
        return pltpu.make_async_remote_copy(
            src_ref=p_out.at[:, lanes(s * CH, n)],
            dst_ref=halo_p.at[par, :, lanes(s * CH, n)],
            send_sem=ps_sem.at[s],
            recv_sem=pr_sem.at[par, s],
            device_id=(m - 1, v),
            device_id_type=MESH,
        )

    def start_u(par, s):
        @pl.when(m < nm - 1)
        def _():
            send_u(par, s).start()

    def start_p(par, s):
        @pl.when(m > 0)
        def _():
            send_p(par, s).start()

    def wait_halo(par, s, sends=True):
        @pl.when(m > 0)
        def _():
            send_u(par, s).wait_recv()
            send_p(par, s).wait_send()

        @pl.when(m < nm - 1)
        def _():
            send_p(par, s).wait_recv()
            send_u(par, s).wait_send()

    def row_scale(q):
        b = block_of(q)
        return scale[b : b + 1, :]

    def products_down(s):
        for p in range(s * CH, (s + 1) * CH):
            b = block_of(p)
            up = u[:, lanes(p)]
            p_out[:, lanes(p)] = dot(up, far[b], NN).astype(BF16)
            if b == 0:
                p_out[:, lanes(HALF)] = dot(up, near[0], NN).astype(BF16)

    def local_terms(q):
        b = block_of(q)
        at = lambda c: u[:, lanes(place_of(c))]
        if b < HALF:
            if b > 0:
                total = dot(
                    jnp.concatenate([at(b - 1), at(b)], axis=1),
                    jnp.concatenate([near[b], diag[b]], axis=1), NT)
            else:
                total = dot(at(b), diag[b], NT)
            total += dot(
                jnp.concatenate([at(b + 1), at(b + HALF)], axis=1),
                jnp.concatenate([near[b + 1], far[b + HALF]], axis=0), NN)
        else:
            total = dot(
                jnp.concatenate([at(b - 1), at(b - HALF)], axis=1),
                jnp.concatenate([near[b], far[b]], axis=1), NT)
            if b < 2 * HALF - 1:
                total += dot(
                    jnp.concatenate([at(b), at(b + 1)], axis=1),
                    jnp.concatenate([diag[b], near[b + 1]], axis=0), NN)
            else:
                total += dot(at(b), diag[b], NN)
        acc[:, lanes(q)] = total

    def local_places(s):
        if s == 0:
            places = range(1, CH - 1)
        elif s < STEPS - 1:
            places = range(s * CH - 1, (s + 1) * CH - 1)
        else:
            places = [*range(s * CH - 1, HALF), 0]
        return places

    def local_step(s):
        for p in local_places(s):
            local_terms(p)
            local_terms(HALF + p)

    def upper_total(par, q):
        p = q - HALF
        total = acc[:, lanes(q)] + halo_p[par, :, lanes(p)].astype(F32)
        if block_of(q) == 2 * HALF - 1:
            total += halo_p[par, :, lanes(HALF)].astype(F32)
        return total

    def lower_total(par, p):
        b = block_of(p)
        if b == 0:
            far_term = dot(
                jnp.concatenate([halo_u[par, :, lanes(p)], halo_u[par, :, lanes(p - 1)]], axis=1),
                jnp.concatenate([far[b], near[b]], axis=1), NT)
        else:
            far_term = dot(halo_u[par, :, lanes(p)], far[b], NT)
        return acc[:, lanes(p)] + far_term

    def recur(q, total, now, weight, fresh):
        image = row_scale(q) * total
        current = x[now, :, lanes(q)]
        before = x[1 - now, :, lanes(q)]
        following = weight * (image - CENTER * current) - jnp.where(fresh, 0.0, before)
        x[1 - now, :, lanes(q)] = following
        u[:, lanes(q)] = (row_scale(q) * following).astype(BF16)
        return following

    def deal(q, value, box):
        p = q % HALF
        s, r = p // CH, p % CH
        per = CH // nv
        box[s, r // per, :, lanes((q // HALF) * per + r % per)] = value.astype(BF16)

    def exchange(box, whole, ss, rs, s, d):
        to = lax.rem(v + d, nv)
        return pltpu.make_async_remote_copy(
            src_ref=box.at[s, to],
            dst_ref=whole.at[s, pl.ds(pl.multiple_of(32 * v, 32), 32), :],
            send_sem=ss.at[d - 1, s],
            recv_sem=rs.at[d - 1, s],
            device_id=(m, to),
            device_id_type=MESH,
        )

    def spread(box, whole, ss, rs, s):
        for d in (2, 1, 3):
            exchange(box, whole, ss, rs, s, d).start()
        whole[s, pl.ds(pl.multiple_of(32 * v, 32), 32), :] = box[s, v]

    def out_copy(h, r):
        pos, blk, n = RUNS[r]
        return pltpu.make_async_copy(
            x.at[0, :, lanes(h * HALF + pos, n)],
            out_hbm.at[:, lanes(h * HALF + blk, n)],
            o_sem.at[h, r],
        )

    for s in range(STEPS):
        for r in runs_of(s):
            x_copy(1, r).wait()
        for q in range(HALF + s * CH, HALF + (s + 1) * CH):
            u[:, lanes(q)] = (row_scale(q) * x[0, :, lanes(q)]).astype(BF16)
        start_u(0, s)
        for r in runs_of(s):
            x_copy(0, r).wait()
            far_copy(r).wait()
        for p in range(s * CH, (s + 1) * CH):
            u[:, lanes(p)] = (row_scale(p) * x[0, :, lanes(p)]).astype(BF16)
        if s == STEPS - 1:
            mats[2].wait()
        products_down(s)
        start_p(0, s)
    mats[0].wait()
    mats[1].wait()
    for s in range(STEPS):
        local_step(s)

    def operation(k, last):
        par = lax.rem(k, 2)
        nxt = 1 - par
        fresh = lax.rem(k, DEGREE) == 0
        weight = jnp.where(fresh, 0.125, 0.25).astype(F32)
        for s in range(STEPS):
            wait_halo(par, s)
            for q in range(HALF + s * CH, HALF + (s + 1) * CH):
                value = recur(q, upper_total(par, q), par, weight, fresh)
                if last:
                    deal(q, value, f_out)
            start_u(nxt, s)
            for p in range(s * CH, (s + 1) * CH):
                value = recur(p, lower_total(par, p), par, weight, fresh)
                if last:
                    deal(p, value, f_out)
            products_down(s)
            start_p(nxt, s)
            if last:
                spread(f_out, f_all, fs_sem, fr_sem, s)
                for r in runs_of(s):
                    out_copy(0, r).start()
                    out_copy(1, r).start()
            local_step(s)

    def loop_body(k, carry):
        operation(k, False)
        return carry

    lax.fori_loop(0, NOPS - 1, loop_body, 0)
    operation(NOPS - 1, True)

    for s in range(STEPS):
        wait_halo(NOPS % 2, s)
        for q in range(HALF + s * CH, HALF + (s + 1) * CH):
            deal(q, row_scale(q) * upper_total(NOPS % 2, q), g_out)
        for p in range(s * CH, (s + 1) * CH):
            deal(p, row_scale(p) * lower_total(NOPS % 2, p), g_out)
        spread(g_out, g_all, gs_sem, gr_sem, s)

    for s in range(STEPS):
        for d in range(1, nv):
            exchange(f_out, f_all, fs_sem, fr_sem, s, d).wait()
        part = dot(f_all[s], f_all[s], NT)
        q_buf[1] = part if s == 0 else q_buf[1] + part
    for s in range(STEPS):
        for d in range(1, nv):
            exchange(g_out, g_all, gs_sem, gr_sem, s, d).wait()
        part = dot(g_all[s], f_all[s], NT)
        q_buf[0] = part if s == 0 else q_buf[0] + part

    width = 128 // nm
    for i in range(nm):
        t_buf[i, 0:width, :] = q_buf[0, i * width : (i + 1) * width, :]
        t_buf[i, width : 2 * width, :] = q_buf[1, i * width : (i + 1) * width, :]

    def fold(d):
        to = lax.rem(m + d, nm)
        return pltpu.make_async_remote_copy(
            src_ref=t_buf.at[to],
            dst_ref=r_buf.at[d - 1],
            send_sem=ts_sem.at[d - 1],
            recv_sem=tr_sem.at[d - 1],
            device_id=(to, v),
            device_id_type=MESH,
        )

    def fold_start(d, carry):
        fold(d).start()
        return carry

    def fold_wait(d, carry):
        fold(d).wait()
        return carry + r_buf[d - 1]

    lax.fori_loop(1, nm, fold_start, 0)
    s_buf[...] = lax.fori_loop(1, nm, fold_wait, t_buf[m])

    def fold_vec(d):
        return pltpu.make_async_remote_copy(
            src_ref=s_buf,
            dst_ref=r2_buf.at[d - 1],
            send_sem=s2_sem.at[d - 1],
            recv_sem=r2_sem.at[d - 1],
            device_id=(m, lax.rem(v + d, nv)),
            device_id_type=MESH,
        )

    for d in range(1, nv):
        fold_vec(d).start()
    total = s_buf[...]
    for d in range(1, nv):
        fold_vec(d).wait()
        total = total + r2_buf[d - 1]
    cols = 128 // nv
    mine = jnp.zeros((2 * width, cols), F32)
    for j in range(nv):
        mine = jnp.where(v == j, total[:, j * cols : (j + 1) * cols], mine)
    stiff_ref[...] = mine[0:width]
    massg_ref[...] = mine[width : 2 * width]

    for h in range(2):
        for r in range(NRUN):
            out_copy(h, r).wait()


def shards(nm, nv, panel, orient, mass, stiff_diag, near_coupling, far_coupling):
    rows, columns = panel.shape
    blocks = stiff_diag.shape[0]
    width = 128 // nm
    anywhere = pl.BlockSpec(memory_space=pl.ANY)
    inside = pl.BlockSpec(memory_space=pltpu.VMEM)
    dma = pltpu.SemaphoreType.DMA
    mat = pltpu.VMEM((blocks, BS, BS), BF16)
    scratch = [
        pltpu.VMEM((blocks, BS), jnp.int32),
        pltpu.VMEM((blocks, BS), F32),
        pltpu.VMEM((blocks, BS), F32),
        mat, mat, mat,
        pltpu.VMEM((2, columns, rows), F32),
        pltpu.VMEM((columns, rows), F32),
        pltpu.VMEM((columns, rows), BF16),
        pltpu.VMEM((2, columns, HALF * BS), BF16),
        pltpu.VMEM((columns, (HALF + 1) * BS), BF16),
        pltpu.VMEM((2, columns, (HALF + 1) * BS), BF16),
        pltpu.VMEM((STEPS, nv, columns, rows // STEPS // nv), BF16),
        pltpu.VMEM((STEPS, nv, columns, rows // STEPS // nv), BF16),
        pltpu.VMEM((STEPS, nv * columns, rows // STEPS // nv), BF16),
        pltpu.VMEM((STEPS, nv * columns, rows // STEPS // nv), BF16),
        pltpu.VMEM((2, 128, 128), F32),
        pltpu.VMEM((nm, 2 * width, 128), F32),
        pltpu.VMEM((nm - 1, 2 * width, 128), F32),
        pltpu.VMEM((2 * width, 128), F32),
        pltpu.VMEM((nv - 1, 2 * width, 128), F32),
        dma((2,)), dma((2, NRUN)), dma((NRUN,)), dma((3,)), dma((2, NRUN)),
        dma((STEPS,)), dma((2, STEPS)), dma((STEPS,)), dma((2, STEPS)),
        dma((nv - 1, STEPS)), dma((nv - 1, STEPS)), dma((nv - 1, STEPS)), dma((nv - 1, STEPS)),
        dma((nm - 1,)), dma((nm - 1,)), dma((nv - 1,)), dma((nv - 1,)),
    ]
    filtered, stiff, massg = pl.pallas_call(
        functools.partial(kernel, nm, nv),
        out_shape=(
            jax.ShapeDtypeStruct((columns, rows), F32),
            jax.ShapeDtypeStruct((width, 128 // nv), F32),
            jax.ShapeDtypeStruct((width, 128 // nv), F32),
        ),
        in_specs=[anywhere] * 6,
        out_specs=(anywhere, inside, inside),
        scratch_shapes=scratch,
        compiler_params=pltpu.CompilerParams(collective_id=0, has_side_effects=True),
        name="filter_ritz",
    )(
        panel.T,
        orient.reshape(blocks, BS),
        mass.reshape(blocks, BS),
        stiff_diag,
        near_coupling,
        far_coupling,
    )
    return (filtered.T, stiff.T, massg.T)


def solution(mesh):
    placed = (
        P("mesh", "vec"),
        P("mesh"),
        P("mesh"),
        P("mesh", None, None),
        P("mesh", None, None),
        P("mesh", None, None),
    )
    return jax.shard_map(
        functools.partial(shards, mesh.shape["mesh"], mesh.shape["vec"]),
        mesh=mesh,
        in_specs=placed,
        out_specs=(P("mesh", "vec"), P("vec", "mesh"), P("vec", "mesh")),
        check_vma=False,
    )
```

```python
import functools

import jax
import jax.numpy as jnp
from jax import lax
from jax.experimental import pallas as pl
from jax.experimental.pallas import tpu as pltpu
from jax.sharding import PartitionSpec as P

SPAN = 32
BS = 128
DEGREE = 4
APPS = 2
NOPS = DEGREE * APPS
CENTER = 6.0

HALF = SPAN
STEPS = 4
CH = HALF // STEPS
GROUP = 8
VMEM_LIMIT = 32 * 1024 * 1024

MESH = pl.DeviceIdType.MESH
NT = (((1,), (1,)), ((), ()))
NN = (((1,), (0,)), ((), ()))
F32 = jnp.float32
BF16 = jnp.bfloat16


def block_of(q):
    return HALF * (q // HALF) + (q % HALF + 1) % HALF


def place_of(b):
    return HALF * (b // HALF) + (b % HALF - 1) % HALF


def lanes(q, n=1):
    return slice(q * BS, (q + n) * BS)


def dot(a, b, dims):
    return lax.dot_general(a, b, dims, preferred_element_type=F32)


def pieces():
    runs = []
    for s in range(STEPS):
        count = CH if s < STEPS - 1 else CH - 1
        runs.append((s * CH, s * CH + 1, count))
    runs.append((HALF - 1, 0, 1))
    return runs


RUNS = pieces()
NRUN = len(RUNS)


def runs_of(s):
    return (s,) if s < STEPS - 1 else (s, s + 1)


def kernel(
    nm, nv,
    x_hbm, orient_hbm, mass_hbm, diag_hbm, near_hbm, far_hbm,
    out_hbm, ritz_ref,
    orient, mass, scale, pair, side, far,
    x, acc, u, halo_u, p_out, halo_p,
    f_out, g_out, f_all, g_all, q_buf, t_buf, ra_buf, sa_buf, rb_buf, sb_buf, rc_buf,
    vec_sem, x_sem, far_sem, mat_sem, o_sem,
    us_sem, ur_sem, ps_sem, pr_sem,
    fs_sem, fr_sem, gs_sem, gr_sem,
    as_sem, ar_sem, bs_sem, br_sem, cs_sem, cr_sem,
):
    m = lax.axis_index("mesh")
    v = lax.axis_index("vec")

    cp_or = pltpu.make_async_copy(orient_hbm, orient, vec_sem.at[0])
    cp_ma = pltpu.make_async_copy(mass_hbm, mass, vec_sem.at[1])
    cp_or.start()
    cp_ma.start()

    def x_copy(h, r):
        pos, blk, n = RUNS[r]
        return pltpu.make_async_copy(
            x_hbm.at[:, lanes(h * HALF + blk, n)],
            x.at[0, :, lanes(h * HALF + pos, n)],
            x_sem.at[h, r],
        )

    def far_copy(r):
        _, blk, n = RUNS[r]
        return pltpu.make_async_copy(far_hbm.at[pl.ds(blk, n)], far.at[pl.ds(blk, n)], far_sem.at[r])

    for r in range(NRUN):
        x_copy(0, r).start()
        x_copy(1, r).start()
        far_copy(r).start()

    lo, hi = pl.ds(0, BS), pl.ds(BS, BS)
    first, second = pl.ds(0, HALF), pl.ds(HALF, HALF)
    mats = [
        pltpu.make_async_copy(near_hbm, side.at[:, :, lo], mat_sem.at[0]),
        pltpu.make_async_copy(far_hbm.at[second], pair.at[:, hi, lo], mat_sem.at[1]),
        pltpu.make_async_copy(diag_hbm.at[first], pair.at[:, lo, lo], mat_sem.at[2]),
        pltpu.make_async_copy(diag_hbm.at[second], pair.at[:, hi, hi], mat_sem.at[3]),
    ]
    for c in mats:
        c.start()

    group = lax.div(m, GROUP)
    member = lax.rem(m, GROUP)
    ngroup = nm // GROUP
    up, down = lax.rem(m + 1, nm), lax.rem(m + nm - 1, nm)

    def in_group(d):
        return group * GROUP + lax.rem(member + d, GROUP)

    def in_column(d):
        return lax.rem(group + d, ngroup) * GROUP + member

    barrier = pltpu.get_barrier_semaphore()
    greeted = [(up, v), (down, v)]
    greeted += [(in_group(d), v) for d in range(1, GROUP)]
    greeted += [(in_column(d), v) for d in range(1, ngroup)]
    greeted += [(m, lax.rem(v + d, nv)) for d in range(1, nv)]
    for peer in greeted:
        pl.semaphore_signal(barrier, inc=1, device_id=peer, device_id_type=MESH)

    cp_or.wait()
    cp_ma.wait()
    scale[...] = orient[...].astype(F32) / jnp.sqrt(mass[...])

    pl.semaphore_wait(barrier, len(greeted))

    def send_u(par, s):
        return pltpu.make_async_remote_copy(
            src_ref=u.at[:, lanes(HALF + s * CH, CH)],
            dst_ref=halo_u.at[par, :, lanes(s * CH, CH)],
            send_sem=us_sem.at[s],
            recv_sem=ur_sem.at[par, s],
            device_id=(up, v),
            device_id_type=MESH,
        )

    def send_p(par, s):
        n = CH + (s == STEPS - 1)
        return pltpu.make_async_remote_copy(
            src_ref=p_out.at[:, lanes(s * CH, n)],
            dst_ref=halo_p.at[par, :, lanes(s * CH, n)],
            send_sem=ps_sem.at[s],
            recv_sem=pr_sem.at[par, s],
            device_id=(down, v),
            device_id_type=MESH,
        )

    def wait_halo(par, s):
        send_u(par, s).wait()
        send_p(par, s).wait()

    has_below = m > 0
    has_above = m < nm - 1

    def row_scale(q):
        b = block_of(q)
        return scale[b : b + 1, :]

    def products_down(s):
        for p in range(s * CH, (s + 1) * CH):
            b = block_of(p)
            mine = u[:, lanes(p)]
            p_out[:, lanes(p)] = dot(mine, far[b], NN).astype(BF16)
            if b == 0:
                p_out[:, lanes(HALF)] = dot(mine, side[0, :, 0:BS], NN).astype(BF16)

    def local_step(s, done, waiting):
        def give(q, value):
            if q in done:
                acc[:, lanes(q)] += value
            elif q in waiting:
                waiting[q] += value
            else:
                waiting[q] = value

        own = []
        for p in range(s * CH, (s + 1) * CH):
            b = block_of(p)
            both = dot(jnp.concatenate([u[:, lanes(p)], u[:, lanes(HALF + p)]], axis=1), pair[b], NN)
            give(p, both[:, 0:BS])
            give(HALF + p, both[:, BS : 2 * BS])
            own += [p, HALF + p]
            for q in (p, HALF + p):
                b = block_of(q)
                beside = dot(u[:, lanes(q)], side[b], NN)
                if b > 0:
                    give(place_of(b - 1), beside[:, 0:BS])
                if b < 2 * HALF - 1:
                    give(place_of(b + 1), beside[:, BS : 2 * BS])
        for q in own:
            acc[:, lanes(q)] = waiting.pop(q)
            done.add(q)

    def local_all():
        done, waiting = set(), {}
        for s in range(STEPS):
            yield functools.partial(local_step, s, done, waiting)

    def upper_total(par, q):
        p = q - HALF
        other = halo_p[par, :, lanes(p)].astype(F32)
        if block_of(q) == 2 * HALF - 1:
            other += halo_p[par, :, lanes(HALF)].astype(F32)
        return acc[:, lanes(q)] + jnp.where(has_above, other, 0.0)

    def lower_total(par, p):
        b = block_of(p)
        if b == 0:
            far_term = dot(
                jnp.concatenate([halo_u[par, :, lanes(p)], halo_u[par, :, lanes(p - 1)]], axis=1),
                jnp.concatenate([far[b], side[b, :, 0:BS]], axis=1), NT)
        else:
            far_term = dot(halo_u[par, :, lanes(p)], far[b], NT)
        return acc[:, lanes(p)] + jnp.where(has_below, far_term, 0.0)

    def recur(q, total, now, weight, fresh):
        image = row_scale(q) * total
        current = x[now, :, lanes(q)]
        before = x[1 - now, :, lanes(q)]
        following = weight * (image - CENTER * current) - jnp.where(fresh, 0.0, before)
        x[1 - now, :, lanes(q)] = following
        u[:, lanes(q)] = (row_scale(q) * following).astype(BF16)
        return following

    def deal(q, value, box):
        p = q % HALF
        s, r = p // CH, p % CH
        per = CH // nv
        box[s, r // per, :, lanes((q // HALF) * per + r % per)] = value.astype(BF16)

    def exchange(box, whole, ss, rs, s, d):
        to = lax.rem(v + d, nv)
        return pltpu.make_async_remote_copy(
            src_ref=box.at[s, to],
            dst_ref=whole.at[s, pl.ds(pl.multiple_of(32 * v, 32), 32), :],
            send_sem=ss.at[d - 1, s],
            recv_sem=rs.at[d - 1, s],
            device_id=(m, to),
            device_id_type=MESH,
        )

    def spread(box, whole, ss, rs, s):
        for d in (2, 1, 3):
            exchange(box, whole, ss, rs, s, d).start()
        whole[s, pl.ds(pl.multiple_of(32 * v, 32), 32), :] = box[s, v]

    def out_copy(h, r):
        pos, blk, n = RUNS[r]
        return pltpu.make_async_copy(
            x.at[0, :, lanes(h * HALF + pos, n)],
            out_hbm.at[:, lanes(h * HALF + blk, n)],
            o_sem.at[h, r],
        )

    for s in range(STEPS):
        for r in runs_of(s):
            x_copy(1, r).wait()
        for q in range(HALF + s * CH, HALF + (s + 1) * CH):
            u[:, lanes(q)] = (row_scale(q) * x[0, :, lanes(q)]).astype(BF16)
        send_u(0, s).start()
        for r in runs_of(s):
            x_copy(0, r).wait()
            far_copy(r).wait()
        for p in range(s * CH, (s + 1) * CH):
            u[:, lanes(p)] = (row_scale(p) * x[0, :, lanes(p)]).astype(BF16)
        if s == STEPS - 1:
            mats[0].wait()
        products_down(s)
        send_p(0, s).start()
    for c in mats[1:]:
        c.wait()

    def turn(b, carry):
        pair[b, 0:BS, BS : 2 * BS] = pair[b, BS : 2 * BS, 0:BS].T
        side[2 * b, :, BS : 2 * BS] = side[2 * b + 1, :, 0:BS].T
        side[2 * b + 1, :, BS : 2 * BS] = side[jnp.minimum(2 * b + 2, 2 * HALF - 1), :, 0:BS].T
        return carry

    lax.fori_loop(0, HALF, turn, 0, unroll=2)
    for step in local_all():
        step()

    def operation(k, last):
        par = lax.rem(k, 2)
        nxt = 1 - par
        fresh = lax.rem(k, DEGREE) == 0
        weight = jnp.where(fresh, 0.125, 0.25).astype(F32)
        local = list(local_all())
        for s in range(STEPS):
            wait_halo(par, s)
            for q in range(HALF + s * CH, HALF + (s + 1) * CH):
                value = recur(q, upper_total(par, q), par, weight, fresh)
                if last:
                    deal(q, value, f_out)
            send_u(nxt, s).start()
            for p in range(s * CH, (s + 1) * CH):
                value = recur(p, lower_total(par, p), par, weight, fresh)
                if last:
                    deal(p, value, f_out)
            products_down(s)
            send_p(nxt, s).start()
            if last:
                spread(f_out, f_all, fs_sem, fr_sem, s)
                for r in runs_of(s):
                    out_copy(0, r).start()
                    out_copy(1, r).start()
            local[s]()

    def loop_body(k, carry):
        operation(k, False)
        return carry

    lax.fori_loop(0, NOPS - 1, loop_body, 0)
    operation(NOPS - 1, True)

    for s in range(STEPS):
        wait_halo(NOPS % 2, s)
        for q in range(HALF + s * CH, HALF + (s + 1) * CH):
            deal(q, row_scale(q) * upper_total(NOPS % 2, q), g_out)
        for p in range(s * CH, (s + 1) * CH):
            deal(p, row_scale(p) * lower_total(NOPS % 2, p), g_out)
        spread(g_out, g_all, gs_sem, gr_sem, s)

    for s in range(STEPS):
        for d in range(1, nv):
            exchange(f_out, f_all, fs_sem, fr_sem, s, d).wait()
        part = dot(f_all[s], f_all[s], NT)
        q_buf[1] = part if s == 0 else q_buf[1] + part
    for s in range(STEPS):
        for d in range(1, nv):
            exchange(g_out, g_all, gs_sem, gr_sem, s, d).wait()
        part = dot(g_all[s], f_all[s], NT)
        q_buf[0] = part if s == 0 else q_buf[0] + part

    width = 128 // nm
    for i in range(nm):
        t_buf[i % GROUP, i // GROUP, 0:width, :] = q_buf[0, i * width : (i + 1) * width, :]
        t_buf[i % GROUP, i // GROUP, width : 2 * width, :] = q_buf[1, i * width : (i + 1) * width, :]

    def fold(source, box, ss, rs, d, peer):
        return pltpu.make_async_remote_copy(
            src_ref=source, dst_ref=box.at[d - 1], send_sem=ss.at[d - 1], recv_sem=rs.at[d - 1],
            device_id=peer, device_id_type=MESH)

    def fold_a(d):
        return fold(t_buf.at[lax.rem(member + d, GROUP)], ra_buf, as_sem, ar_sem, d, (in_group(d), v))

    def fold_b(d):
        return fold(sa_buf.at[lax.rem(group + d, ngroup)], rb_buf, bs_sem, br_sem, d, (in_column(d), v))

    def fold_c(d):
        return fold(sb_buf, rc_buf, cs_sem, cr_sem, d, (m, lax.rem(v + d, nv)))

    for d in range(1, GROUP):
        fold_a(d).start()
    total = t_buf[member]
    for d in range(1, GROUP):
        fold_a(d).wait()
        total = total + ra_buf[d - 1]
    sa_buf[...] = total
    for d in range(1, ngroup):
        fold_b(d).start()
    total = sa_buf[group]
    for d in range(1, ngroup):
        fold_b(d).wait()
        total = total + rb_buf[d - 1]
    sb_buf[...] = total
    for d in range(1, nv):
        fold_c(d).start()
    for d in range(1, nv):
        fold_c(d).wait()
        total = total + rc_buf[d - 1]
    cols = 128 // nv
    mine = jnp.zeros((2 * width, cols), F32)
    for j in range(nv):
        mine = jnp.where(v == j, total[:, j * cols : (j + 1) * cols], mine)
    ritz_ref[...] = mine

    for h in range(2):
        for r in range(NRUN):
            out_copy(h, r).wait()


def write_out(filtered, ritz, out, stiff, massg, sem):
    copy = pltpu.make_async_copy(filtered, out, sem)
    copy.start()
    width = stiff.shape[0]
    stiff[...] = ritz[0:width]
    massg[...] = ritz[width : 2 * width]
    copy.wait()


def shards(nm, nv, panel, orient, mass, stiff_diag, near_coupling, far_coupling):
    rows, columns = panel.shape
    blocks = stiff_diag.shape[0]
    width = 128 // nm
    cols = 128 // nv
    ngroup = nm // GROUP
    anywhere = pl.BlockSpec(memory_space=pl.ANY)
    inside = pl.BlockSpec(memory_space=pltpu.VMEM)
    dma = pltpu.SemaphoreType.DMA
    dealt = rows // STEPS // nv
    scratch = [
        pltpu.VMEM((blocks, BS), jnp.int32),
        pltpu.VMEM((blocks, BS), F32),
        pltpu.VMEM((blocks, BS), F32),
        pltpu.VMEM((HALF, 2 * BS, 2 * BS), BF16),
        pltpu.VMEM((blocks, BS, 2 * BS), BF16),
        pltpu.VMEM((HALF, BS, BS), BF16),
        pltpu.VMEM((2, columns, rows), F32),
        pltpu.VMEM((columns, rows), F32),
        pltpu.VMEM((columns, rows), BF16),
        pltpu.VMEM((2, columns, HALF * BS), BF16),
        pltpu.VMEM((columns, (HALF + 1) * BS), BF16),
        pltpu.VMEM((2, columns, (HALF + 1) * BS), BF16),
        pltpu.VMEM((STEPS, nv, columns, dealt), BF16),
        pltpu.VMEM((STEPS, nv, columns, dealt), BF16),
        pltpu.VMEM((STEPS, nv * columns, dealt), BF16),
        pltpu.VMEM((STEPS, nv * columns, dealt), BF16),
        pltpu.VMEM((2, 128, 128), F32),
        pltpu.VMEM((GROUP, ngroup, 2 * width, 128), F32),
        pltpu.VMEM((GROUP - 1, ngroup, 2 * width, 128), F32),
        pltpu.VMEM((ngroup, 2 * width, 128), F32),
        pltpu.VMEM((ngroup - 1, 2 * width, 128), F32),
        pltpu.VMEM((2 * width, 128), F32),
        pltpu.VMEM((nv - 1, 2 * width, 128), F32),
        dma((2,)), dma((2, NRUN)), dma((NRUN,)), dma((4,)), dma((2, NRUN)),
        dma((STEPS,)), dma((2, STEPS)), dma((STEPS,)), dma((2, STEPS)),
        dma((nv - 1, STEPS)), dma((nv - 1, STEPS)), dma((nv - 1, STEPS)), dma((nv - 1, STEPS)),
        dma((GROUP - 1,)), dma((GROUP - 1,)), dma((ngroup - 1,)), dma((ngroup - 1,)), dma((nv - 1,)), dma((nv - 1,)),
    ]
    filtered, ritz = pl.pallas_call(
        functools.partial(kernel, nm, nv),
        out_shape=(
            jax.ShapeDtypeStruct((columns, rows), F32),
            jax.ShapeDtypeStruct((2 * width, cols), F32),
        ),
        in_specs=[pl.BlockSpec(memory_space=pltpu.HBM)] * 6,
        out_specs=(anywhere, inside),
        scratch_shapes=scratch,
        compiler_params=pltpu.CompilerParams(
            collective_id=0, has_side_effects=True, vmem_limit_bytes=VMEM_LIMIT),
        name="filter_ritz",
    )(*[
        pltpu.with_memory_space_constraint(a, pltpu.HBM)
        for a in (
            panel.T,
            orient.reshape(blocks, BS),
            mass.reshape(blocks, BS),
            stiff_diag,
            near_coupling,
            far_coupling,
        )
    ])
    filtered, stiff, massg = pl.pallas_call(
        write_out,
        out_shape=(
            jax.ShapeDtypeStruct((columns, rows), F32),
            jax.ShapeDtypeStruct((width, cols), F32),
            jax.ShapeDtypeStruct((width, cols), F32),
        ),
        in_specs=[inside, inside],
        out_specs=(anywhere, inside, inside),
        scratch_shapes=[pltpu.SemaphoreType.DMA],
        compiler_params=pltpu.CompilerParams(vmem_limit_bytes=VMEM_LIMIT),
        name="write_out",
    )(filtered, ritz)
    return (filtered.T, stiff.T, massg.T)


def solution(mesh):
    placed = (
        P("mesh", "vec"),
        P("mesh"),
        P("mesh"),
        P("mesh", None, None),
        P("mesh", None, None),
        P("mesh", None, None),
    )
    return jax.shard_map(
        functools.partial(shards, mesh.shape["mesh"], mesh.shape["vec"]),
        mesh=mesh,
        in_specs=placed,
        out_specs=(P("mesh", "vec"), P("vec", "mesh"), P("vec", "mesh")),
        check_vma=False,
    )
```

```python
import functools

import jax
import jax.numpy as jnp
from jax import lax
from jax.experimental import pallas as pl
from jax.experimental.pallas import tpu as pltpu
from jax.sharding import PartitionSpec as P

SPAN = 32
BS = 128
DEGREE = 4
APPS = 2
NOPS = DEGREE * APPS
CENTER = 6.0

HALF = SPAN
STEPS = 4
CH = HALF // STEPS
VMEM_LIMIT = 32 * 1024 * 1024

MESH = pl.DeviceIdType.MESH
NT = (((1,), (1,)), ((), ()))
NN = (((1,), (0,)), ((), ()))
F32 = jnp.float32
BF16 = jnp.bfloat16


def block_of(q):
    return HALF * (q // HALF) + (q % HALF + 1) % HALF


def place_of(b):
    return HALF * (b // HALF) + (b % HALF - 1) % HALF


def lanes(q, n=1):
    return slice(q * BS, (q + n) * BS)


def dot(a, b, dims):
    return lax.dot_general(a, b, dims, preferred_element_type=F32)


def pieces():
    runs = []
    for s in range(STEPS):
        count = CH if s < STEPS - 1 else CH - 1
        runs.append((s * CH, s * CH + 1, count))
    runs.append((HALF - 1, 0, 1))
    return runs


RUNS = pieces()
NRUN = len(RUNS)


def runs_of(s):
    return (s,) if s < STEPS - 1 else (s, s + 1)


def kernel(
    nm, nv,
    x_hbm, orient_hbm, mass_hbm, diag_hbm, near_hbm, far_hbm,
    out_hbm, ritz_ref,
    orient, mass, scale, diag, near, far,
    x, acc, u, halo_u, p_out, halo_p,
    f_out, g_out, f_all, g_all, q_buf, t_buf, r_buf, s_buf, r2_buf,
    vec_sem, x_sem, far_sem, mat_sem, o_sem,
    us_sem, ur_sem, ps_sem, pr_sem,
    fs_sem, fr_sem, gs_sem, gr_sem,
    ts_sem, tr_sem, s2_sem, r2_sem,
):
    m = lax.axis_index("mesh")
    v = lax.axis_index("vec")

    cp_or = pltpu.make_async_copy(orient_hbm, orient, vec_sem.at[0])
    cp_ma = pltpu.make_async_copy(mass_hbm, mass, vec_sem.at[1])
    cp_or.start()
    cp_ma.start()

    def x_copy(h, r):
        pos, blk, n = RUNS[r]
        return pltpu.make_async_copy(
            x_hbm.at[:, lanes(h * HALF + blk, n)],
            x.at[0, :, lanes(h * HALF + pos, n)],
            x_sem.at[h, r],
        )

    def far_copy(r):
        _, blk, n = RUNS[r]
        return pltpu.make_async_copy(far_hbm.at[pl.ds(blk, n)], far.at[pl.ds(blk, n)], far_sem.at[r])

    for r in range(NRUN):
        x_copy(0, r).start()
        x_copy(1, r).start()
        far_copy(r).start()

    mats = [
        pltpu.make_async_copy(far_hbm.at[pl.ds(HALF, HALF)], far.at[pl.ds(HALF, HALF)], mat_sem.at[0]),
        pltpu.make_async_copy(diag_hbm, diag, mat_sem.at[1]),
        pltpu.make_async_copy(near_hbm, near, mat_sem.at[2]),
    ]
    for c in mats:
        c.start()

    @pl.when(m == 0)
    def _():
        halo_u[...] = jnp.zeros_like(halo_u)

    @pl.when(m == nm - 1)
    def _():
        halo_p[...] = jnp.zeros_like(halo_p)

    barrier = pltpu.get_barrier_semaphore()

    def hello_mesh(d, carry):
        pl.semaphore_signal(barrier, inc=1, device_id=(lax.rem(m + d, nm), v), device_id_type=MESH)
        return carry

    lax.fori_loop(1, nm, hello_mesh, 0)
    for d in range(1, nv):
        pl.semaphore_signal(barrier, inc=1, device_id=(m, lax.rem(v + d, nv)), device_id_type=MESH)

    cp_or.wait()
    cp_ma.wait()
    scale[...] = orient[...].astype(F32) / jnp.sqrt(mass[...])

    pl.semaphore_wait(barrier, nm - 1 + nv - 1)

    def send_u(par, s):
        return pltpu.make_async_remote_copy(
            src_ref=u.at[:, lanes(HALF + s * CH, CH)],
            dst_ref=halo_u.at[par, :, lanes(s * CH, CH)],
            send_sem=us_sem.at[s],
            recv_sem=ur_sem.at[par, s],
            device_id=(m + 1, v),
            device_id_type=MESH,
        )

    def send_p(par, s):
        n = CH + (s == STEPS - 1)
        return pltpu.make_async_remote_copy(
            src_ref=p_out.at[:, lanes(s * CH, n)],
            dst_ref=halo_p.at[par, :, lanes(s * CH, n)],
            send_sem=ps_sem.at[s],
            recv_sem=pr_sem.at[par, s],
            device_id=(m - 1, v),
            device_id_type=MESH,
        )

    def start_u(par, s):
        @pl.when(m < nm - 1)
        def _():
            send_u(par, s).start()

    def start_p(par, s):
        @pl.when(m > 0)
        def _():
            send_p(par, s).start()

    def wait_halo(par, s, sends=True):
        @pl.when(m > 0)
        def _():
            send_u(par, s).wait_recv()
            send_p(par, s).wait_send()

        @pl.when(m < nm - 1)
        def _():
            send_p(par, s).wait_recv()
            send_u(par, s).wait_send()

    def row_scale(q):
        b = block_of(q)
        return scale[b : b + 1, :]

    def products_down(s):
        for p in range(s * CH, (s + 1) * CH):
            b = block_of(p)
            up = u[:, lanes(p)]
            p_out[:, lanes(p)] = dot(up, far[b], NN).astype(BF16)
            if b == 0:
                p_out[:, lanes(HALF)] = dot(up, near[0], NN).astype(BF16)

    def local_terms(q):
        b = block_of(q)
        at = lambda c: u[:, lanes(place_of(c))]
        if b < HALF:
            if b > 0:
                total = dot(
                    jnp.concatenate([at(b - 1), at(b)], axis=1),
                    jnp.concatenate([near[b], diag[b]], axis=1), NT)
            else:
                total = dot(at(b), diag[b], NT)
            total += dot(
                jnp.concatenate([at(b + 1), at(b + HALF)], axis=1),
                jnp.concatenate([near[b + 1], far[b + HALF]], axis=0), NN)
        else:
            total = dot(
                jnp.concatenate([at(b - 1), at(b - HALF)], axis=1),
                jnp.concatenate([near[b], far[b]], axis=1), NT)
            if b < 2 * HALF - 1:
                total += dot(
                    jnp.concatenate([at(b), at(b + 1)], axis=1),
                    jnp.concatenate([diag[b], near[b + 1]], axis=0), NN)
            else:
                total += dot(at(b), diag[b], NN)
        acc[:, lanes(q)] = total

    def local_places(s):
        if s == 0:
            places = range(1, CH - 1)
        elif s < STEPS - 1:
            places = range(s * CH - 1, (s + 1) * CH - 1)
        else:
            places = [*range(s * CH - 1, HALF), 0]
        return places

    def local_step(s):
        for p in local_places(s):
            local_terms(p)
            local_terms(HALF + p)

    def upper_total(par, q):
        p = q - HALF
        total = acc[:, lanes(q)] + halo_p[par, :, lanes(p)].astype(F32)
        if block_of(q) == 2 * HALF - 1:
            total += halo_p[par, :, lanes(HALF)].astype(F32)
        return total

    def lower_total(par, p):
        b = block_of(p)
        if b == 0:
            far_term = dot(
                jnp.concatenate([halo_u[par, :, lanes(p)], halo_u[par, :, lanes(p - 1)]], axis=1),
                jnp.concatenate([far[b], near[b]], axis=1), NT)
        else:
            far_term = dot(halo_u[par, :, lanes(p)], far[b], NT)
        return acc[:, lanes(p)] + far_term

    def recur(q, total, now, weight, fresh):
        image = row_scale(q) * total
        current = x[now, :, lanes(q)]
        before = x[1 - now, :, lanes(q)]
        following = weight * (image - CENTER * current) - jnp.where(fresh, 0.0, before)
        x[1 - now, :, lanes(q)] = following
        u[:, lanes(q)] = (row_scale(q) * following).astype(BF16)
        return following

    def deal(q, value, box):
        p = q % HALF
        s, r = p // CH, p % CH
        per = CH // nv
        box[s, r // per, :, lanes((q // HALF) * per + r % per)] = value.astype(BF16)

    def exchange(box, whole, ss, rs, s, d):
        to = lax.rem(v + d, nv)
        return pltpu.make_async_remote_copy(
            src_ref=box.at[s, to],
            dst_ref=whole.at[s, pl.ds(pl.multiple_of(32 * v, 32), 32), :],
            send_sem=ss.at[d - 1, s],
            recv_sem=rs.at[d - 1, s],
            device_id=(m, to),
            device_id_type=MESH,
        )

    def spread(box, whole, ss, rs, s):
        for d in (2, 1, 3):
            exchange(box, whole, ss, rs, s, d).start()
        whole[s, pl.ds(pl.multiple_of(32 * v, 32), 32), :] = box[s, v]

    def out_copy(h, r):
        pos, blk, n = RUNS[r]
        return pltpu.make_async_copy(
            x.at[0, :, lanes(h * HALF + pos, n)],
            out_hbm.at[:, lanes(h * HALF + blk, n)],
            o_sem.at[h, r],
        )

    for s in range(STEPS):
        for r in runs_of(s):
            x_copy(1, r).wait()
        for q in range(HALF + s * CH, HALF + (s + 1) * CH):
            u[:, lanes(q)] = (row_scale(q) * x[0, :, lanes(q)]).astype(BF16)
        start_u(0, s)
        for r in runs_of(s):
            x_copy(0, r).wait()
            far_copy(r).wait()
        for p in range(s * CH, (s + 1) * CH):
            u[:, lanes(p)] = (row_scale(p) * x[0, :, lanes(p)]).astype(BF16)
        if s == STEPS - 1:
            mats[2].wait()
        products_down(s)
        start_p(0, s)
    mats[0].wait()
    mats[1].wait()
    for s in range(STEPS):
        local_step(s)

    def operation(k, last):
        par = lax.rem(k, 2)
        nxt = 1 - par
        fresh = lax.rem(k, DEGREE) == 0
        weight = jnp.where(fresh, 0.125, 0.25).astype(F32)
        for s in range(STEPS):
            wait_halo(par, s)
            for q in range(HALF + s * CH, HALF + (s + 1) * CH):
                value = recur(q, upper_total(par, q), par, weight, fresh)
                if last:
                    deal(q, value, f_out)
            for p in range(s * CH, (s + 1) * CH):
                value = recur(p, lower_total(par, p), par, weight, fresh)
                if last:
                    deal(p, value, f_out)
            products_down(s)
            start_u(nxt, s)
            start_p(nxt, s)
            if last:
                spread(f_out, f_all, fs_sem, fr_sem, s)
                for r in runs_of(s):
                    out_copy(0, r).start()
                    out_copy(1, r).start()
            local_step(s)

    def loop_body(k, carry):
        operation(k, False)
        return carry

    lax.fori_loop(0, NOPS - 1, loop_body, 0)
    operation(NOPS - 1, True)

    for s in range(STEPS):
        wait_halo(NOPS % 2, s)
        for q in range(HALF + s * CH, HALF + (s + 1) * CH):
            deal(q, row_scale(q) * upper_total(NOPS % 2, q), g_out)
        for p in range(s * CH, (s + 1) * CH):
            deal(p, row_scale(p) * lower_total(NOPS % 2, p), g_out)
        spread(g_out, g_all, gs_sem, gr_sem, s)

    for s in range(STEPS):
        for d in range(1, nv):
            exchange(f_out, f_all, fs_sem, fr_sem, s, d).wait_recv()
        part = dot(f_all[s], f_all[s], NT)
        q_buf[1] = part if s == 0 else q_buf[1] + part
    for s in range(STEPS):
        for d in range(1, nv):
            exchange(g_out, g_all, gs_sem, gr_sem, s, d).wait_recv()
        part = dot(g_all[s], f_all[s], NT)
        q_buf[0] = part if s == 0 else q_buf[0] + part

    width = 128 // nm
    for i in range(nm):
        t_buf[i, 0:width, :] = q_buf[0, i * width : (i + 1) * width, :]
        t_buf[i, width : 2 * width, :] = q_buf[1, i * width : (i + 1) * width, :]

    def fold(d):
        to = lax.rem(m + d, nm)
        return pltpu.make_async_remote_copy(
            src_ref=t_buf.at[to],
            dst_ref=r_buf.at[d - 1],
            send_sem=ts_sem.at[d - 1],
            recv_sem=tr_sem.at[d - 1],
            device_id=(to, v),
            device_id_type=MESH,
        )

    def fold_start(d, carry):
        fold(d).start()
        return carry

    def fold_wait(d, carry):
        fold(d).wait_recv()
        return carry + r_buf[d - 1]

    lax.fori_loop(1, nm, fold_start, 0)
    s_buf[...] = lax.fori_loop(1, nm, fold_wait, t_buf[m])

    def fold_vec(d):
        return pltpu.make_async_remote_copy(
            src_ref=s_buf,
            dst_ref=r2_buf.at[d - 1],
            send_sem=s2_sem.at[d - 1],
            recv_sem=r2_sem.at[d - 1],
            device_id=(m, lax.rem(v + d, nv)),
            device_id_type=MESH,
        )

    for d in range(1, nv):
        fold_vec(d).start()
    total = s_buf[...]
    for d in range(1, nv):
        fold_vec(d).wait_recv()
        total = total + r2_buf[d - 1]
    cols = 128 // nv
    mine = jnp.zeros((2 * width, cols), F32)
    for j in range(nv):
        mine = jnp.where(v == j, total[:, j * cols : (j + 1) * cols], mine)
    ritz_ref[...] = mine

    for s in range(STEPS):
        for d in range(1, nv):
            exchange(f_out, f_all, fs_sem, fr_sem, s, d).wait_send()
            exchange(g_out, g_all, gs_sem, gr_sem, s, d).wait_send()

    def fold_left(d, carry):
        fold(d).wait_send()
        return carry

    lax.fori_loop(1, nm, fold_left, 0)
    for d in range(1, nv):
        fold_vec(d).wait_send()
    for h in range(2):
        for r in range(NRUN):
            out_copy(h, r).wait()


def write_out(filtered, ritz, out, stiff, massg, sem):
    copy = pltpu.make_async_copy(filtered, out, sem)
    copy.start()
    width = stiff.shape[0]
    stiff[...] = ritz[0:width]
    massg[...] = ritz[width : 2 * width]
    copy.wait()


def shards(nm, nv, panel, orient, mass, stiff_diag, near_coupling, far_coupling):
    rows, columns = panel.shape
    blocks = stiff_diag.shape[0]
    width = 128 // nm
    cols = 128 // nv
    anywhere = pl.BlockSpec(memory_space=pl.ANY)
    inside = pl.BlockSpec(memory_space=pltpu.VMEM)
    dma = pltpu.SemaphoreType.DMA
    mat = pltpu.VMEM((blocks, BS, BS), BF16)
    scratch = [
        pltpu.VMEM((blocks, BS), jnp.int32),
        pltpu.VMEM((blocks, BS), F32),
        pltpu.VMEM((blocks, BS), F32),
        mat, mat, mat,
        pltpu.VMEM((2, columns, rows), F32),
        pltpu.VMEM((columns, rows), F32),
        pltpu.VMEM((columns, rows), BF16),
        pltpu.VMEM((2, columns, HALF * BS), BF16),
        pltpu.VMEM((columns, (HALF + 1) * BS), BF16),
        pltpu.VMEM((2, columns, (HALF + 1) * BS), BF16),
        pltpu.VMEM((STEPS, nv, columns, rows // STEPS // nv), BF16),
        pltpu.VMEM((STEPS, nv, columns, rows // STEPS // nv), BF16),
        pltpu.VMEM((STEPS, nv * columns, rows // STEPS // nv), BF16),
        pltpu.VMEM((STEPS, nv * columns, rows // STEPS // nv), BF16),
        pltpu.VMEM((2, 128, 128), F32),
        pltpu.VMEM((nm, 2 * width, 128), F32),
        pltpu.VMEM((nm - 1, 2 * width, 128), F32),
        pltpu.VMEM((2 * width, 128), F32),
        pltpu.VMEM((nv - 1, 2 * width, 128), F32),
        dma((2,)), dma((2, NRUN)), dma((NRUN,)), dma((3,)), dma((2, NRUN)),
        dma((STEPS,)), dma((2, STEPS)), dma((STEPS,)), dma((2, STEPS)),
        dma((nv - 1, STEPS)), dma((nv - 1, STEPS)), dma((nv - 1, STEPS)), dma((nv - 1, STEPS)),
        dma((nm - 1,)), dma((nm - 1,)), dma((nv - 1,)), dma((nv - 1,)),
    ]
    filtered, ritz = pl.pallas_call(
        functools.partial(kernel, nm, nv),
        out_shape=(
            jax.ShapeDtypeStruct((columns, rows), F32),
            jax.ShapeDtypeStruct((2 * width, cols), F32),
        ),
        in_specs=[pl.BlockSpec(memory_space=pltpu.HBM)] * 6,
        out_specs=(anywhere, inside),
        scratch_shapes=scratch,
        compiler_params=pltpu.CompilerParams(
            collective_id=0, has_side_effects=True, vmem_limit_bytes=VMEM_LIMIT),
        name="filter_ritz",
    )(*[
        pltpu.with_memory_space_constraint(a, pltpu.HBM)
        for a in (
            panel.T,
            orient.reshape(blocks, BS),
            mass.reshape(blocks, BS),
            stiff_diag,
            near_coupling,
            far_coupling,
        )
    ])
    filtered, stiff, massg = pl.pallas_call(
        write_out,
        out_shape=(
            jax.ShapeDtypeStruct((columns, rows), F32),
            jax.ShapeDtypeStruct((width, cols), F32),
            jax.ShapeDtypeStruct((width, cols), F32),
        ),
        in_specs=[inside, inside],
        out_specs=(anywhere, inside, inside),
        scratch_shapes=[pltpu.SemaphoreType.DMA],
        compiler_params=pltpu.CompilerParams(vmem_limit_bytes=VMEM_LIMIT),
        name="write_out",
    )(filtered, ritz)
    return (filtered.T, stiff.T, massg.T)


def solution(mesh):
    placed = (
        P("mesh", "vec"),
        P("mesh"),
        P("mesh"),
        P("mesh", None, None),
        P("mesh", None, None),
        P("mesh", None, None),
    )
    return jax.shard_map(
        functools.partial(shards, mesh.shape["mesh"], mesh.shape["vec"]),
        mesh=mesh,
        in_specs=placed,
        out_specs=(P("mesh", "vec"), P("vec", "mesh"), P("vec", "mesh")),
        check_vma=False,
    )
```

```python
import functools

import jax
import jax.numpy as jnp
from jax import lax
from jax.experimental import pallas as pl
from jax.experimental.pallas import tpu as pltpu
from jax.sharding import PartitionSpec as P

SPAN = 32
BS = 128
DEGREE = 4
APPS = 2
NOPS = DEGREE * APPS
CENTER = 6.0

HALF = SPAN
STEPS = 4
CH = HALF // STEPS
GROUP = 8
F_WAYS = (2, 1, 3)
G_WAYS = (1, 3)
VMEM_LIMIT = 32 * 1024 * 1024

MESH = pl.DeviceIdType.MESH
NT = (((1,), (1,)), ((), ()))
NN = (((1,), (0,)), ((), ()))
F32 = jnp.float32
BF16 = jnp.bfloat16


def block_of(q):
    return HALF * (q // HALF) + (q % HALF + 1) % HALF


def place_of(b):
    return HALF * (b // HALF) + (b % HALF - 1) % HALF


def lanes(q, n=1):
    return slice(q * BS, (q + n) * BS)


def dot(a, b, dims):
    return lax.dot_general(a, b, dims, preferred_element_type=F32)


def pieces():
    runs = []
    for s in range(STEPS):
        count = CH if s < STEPS - 1 else CH - 1
        runs.append((s * CH, s * CH + 1, count))
    runs.append((HALF - 1, 0, 1))
    return runs


RUNS = pieces()
NRUN = len(RUNS)


def runs_of(s):
    return (s,) if s < STEPS - 1 else (s, s + 1)


def kernel(
    nm, nv,
    x_hbm, orient_hbm, mass_hbm, diag_hbm, near_hbm, far_hbm,
    out_hbm, ritz_ref,
    orient, mass, scale, diag, near, far,
    x, acc, u, halo_u, p_out, halo_p,
    f_out, g_out, f_all, g_all, q_buf, t_buf, r_buf, s_buf, r2_buf,
    vec_sem, x_sem, far_sem, mat_sem, o_sem,
    us_sem, ur_sem, ps_sem, pr_sem,
    fs_sem, fr_sem, gs_sem, gr_sem,
    ts_sem, tr_sem, s2_sem, r2_sem,
):
    m = lax.axis_index("mesh")
    v = lax.axis_index("vec")

    cp_or = pltpu.make_async_copy(orient_hbm, orient, vec_sem.at[0])
    cp_ma = pltpu.make_async_copy(mass_hbm, mass, vec_sem.at[1])
    cp_or.start()
    cp_ma.start()

    def x_copy(h, r):
        pos, blk, n = RUNS[r]
        return pltpu.make_async_copy(
            x_hbm.at[:, lanes(h * HALF + blk, n)],
            x.at[0, :, lanes(h * HALF + pos, n)],
            x_sem.at[h, r],
        )

    def far_copy(r):
        _, blk, n = RUNS[r]
        return pltpu.make_async_copy(far_hbm.at[pl.ds(blk, n)], far.at[pl.ds(blk, n)], far_sem.at[r])

    for r in range(NRUN):
        x_copy(0, r).start()
        x_copy(1, r).start()
        far_copy(r).start()

    mats = [
        pltpu.make_async_copy(far_hbm.at[pl.ds(HALF, HALF)], far.at[pl.ds(HALF, HALF)], mat_sem.at[0]),
        pltpu.make_async_copy(diag_hbm, diag, mat_sem.at[1]),
        pltpu.make_async_copy(near_hbm, near, mat_sem.at[2]),
    ]
    for c in mats:
        c.start()

    @pl.when(m == 0)
    def _():
        halo_u[...] = jnp.zeros_like(halo_u)

    @pl.when(m == nm - 1)
    def _():
        halo_p[...] = jnp.zeros_like(halo_p)

    barrier = pltpu.get_barrier_semaphore()

    group, member, ngroup = lax.div(m, GROUP), lax.rem(m, GROUP), nm // GROUP
    greeted = [(lax.rem(m + 1, nm), v), (lax.rem(m + nm - 1, nm), v)]
    greeted += [(lax.rem(group + d, ngroup) * GROUP + member, v) for d in range(1, ngroup)]
    greeted += [(m, lax.rem(v + d, nv)) for d in range(1, nv)]
    for peer in greeted:
        pl.semaphore_signal(barrier, inc=1, device_id=peer, device_id_type=MESH)

    cp_or.wait()
    cp_ma.wait()
    scale[...] = orient[...].astype(F32) / jnp.sqrt(mass[...])

    pl.semaphore_wait(barrier, len(greeted))

    def send_u(par, s):
        return pltpu.make_async_remote_copy(
            src_ref=u.at[:, lanes(HALF + s * CH, CH)],
            dst_ref=halo_u.at[par, :, lanes(s * CH, CH)],
            send_sem=us_sem.at[s],
            recv_sem=ur_sem.at[par, s],
            device_id=(m + 1, v),
            device_id_type=MESH,
        )

    def send_p(par, s):
        n = CH + (s == STEPS - 1)
        return pltpu.make_async_remote_copy(
            src_ref=p_out.at[:, lanes(s * CH, n)],
            dst_ref=halo_p.at[par, :, lanes(s * CH, n)],
            send_sem=ps_sem.at[s],
            recv_sem=pr_sem.at[par, s],
            device_id=(m - 1, v),
            device_id_type=MESH,
        )

    def start_u(par, s):
        @pl.when(m < nm - 1)
        def _():
            send_u(par, s).start()

    def start_p(par, s):
        @pl.when(m > 0)
        def _():
            send_p(par, s).start()

    def wait_halo(par, s, sends=True):
        @pl.when(m > 0)
        def _():
            send_u(par, s).wait_recv()
            send_p(par, s).wait_send()

        @pl.when(m < nm - 1)
        def _():
            send_p(par, s).wait_recv()
            send_u(par, s).wait_send()

    def row_scale(q):
        b = block_of(q)
        return scale[b : b + 1, :]

    def products_down(s):
        for p in range(s * CH, (s + 1) * CH):
            b = block_of(p)
            up = u[:, lanes(p)]
            p_out[:, lanes(p)] = dot(up, far[b], NN).astype(BF16)
            if b == 0:
                p_out[:, lanes(HALF)] = dot(up, near[0], NN).astype(BF16)

    def local_terms(q):
        b = block_of(q)
        at = lambda c: u[:, lanes(place_of(c))]
        if b < HALF:
            if b > 0:
                total = dot(
                    jnp.concatenate([at(b - 1), at(b)], axis=1),
                    jnp.concatenate([near[b], diag[b]], axis=1), NT)
            else:
                total = dot(at(b), diag[b], NT)
            total += dot(
                jnp.concatenate([at(b + 1), at(b + HALF)], axis=1),
                jnp.concatenate([near[b + 1], far[b + HALF]], axis=0), NN)
        else:
            total = dot(
                jnp.concatenate([at(b - 1), at(b - HALF)], axis=1),
                jnp.concatenate([near[b], far[b]], axis=1), NT)
            if b < 2 * HALF - 1:
                total += dot(
                    jnp.concatenate([at(b), at(b + 1)], axis=1),
                    jnp.concatenate([diag[b], near[b + 1]], axis=0), NN)
            else:
                total += dot(at(b), diag[b], NN)
        acc[:, lanes(q)] = total

    def local_places(s):
        if s == 0:
            places = range(1, CH - 1)
        elif s < STEPS - 1:
            places = range(s * CH - 1, (s + 1) * CH - 1)
        else:
            places = [*range(s * CH - 1, HALF), 0]
        return places

    def local_step(s):
        for p in local_places(s):
            local_terms(p)
            local_terms(HALF + p)

    def upper_total(par, q):
        p = q - HALF
        total = acc[:, lanes(q)] + halo_p[par, :, lanes(p)].astype(F32)
        if block_of(q) == 2 * HALF - 1:
            total += halo_p[par, :, lanes(HALF)].astype(F32)
        return total

    def lower_total(par, p):
        b = block_of(p)
        if b == 0:
            far_term = dot(
                jnp.concatenate([halo_u[par, :, lanes(p)], halo_u[par, :, lanes(p - 1)]], axis=1),
                jnp.concatenate([far[b], near[b]], axis=1), NT)
        else:
            far_term = dot(halo_u[par, :, lanes(p)], far[b], NT)
        return acc[:, lanes(p)] + far_term

    def recur(q, total, now, weight, fresh):
        image = row_scale(q) * total
        current = x[now, :, lanes(q)]
        before = x[1 - now, :, lanes(q)]
        following = weight * (image - CENTER * current) - jnp.where(fresh, 0.0, before)
        x[1 - now, :, lanes(q)] = following
        u[:, lanes(q)] = (row_scale(q) * following).astype(BF16)
        return following

    def deal(q, value, box):
        p = q % HALF
        s, r = p // CH, p % CH
        per = CH // nv
        box[s, r // per, :, lanes((q // HALF) * per + r % per)] = value.astype(BF16)

    def exchange(box, whole, ss, rs, s, d):
        to = lax.rem(v + d, nv)
        return pltpu.make_async_remote_copy(
            src_ref=box.at[s, to],
            dst_ref=whole.at[s, pl.ds(pl.multiple_of(32 * v, 32), 32), :],
            send_sem=ss.at[d - 1, s],
            recv_sem=rs.at[d - 1, s],
            device_id=(m, to),
            device_id_type=MESH,
        )

    def spread(box, whole, ss, rs, s, ways):
        for d in ways:
            exchange(box, whole, ss, rs, s, d).start()
        whole[s, pl.ds(pl.multiple_of(32 * v, 32), 32), :] = box[s, v]

    def out_copy(h, r):
        pos, blk, n = RUNS[r]
        return pltpu.make_async_copy(
            x.at[0, :, lanes(h * HALF + pos, n)],
            out_hbm.at[:, lanes(h * HALF + blk, n)],
            o_sem.at[h, r],
        )

    for s in range(STEPS):
        for r in runs_of(s):
            x_copy(1, r).wait()
        for q in range(HALF + s * CH, HALF + (s + 1) * CH):
            u[:, lanes(q)] = (row_scale(q) * x[0, :, lanes(q)]).astype(BF16)
        start_u(0, s)
        for r in runs_of(s):
            x_copy(0, r).wait()
            far_copy(r).wait()
        for p in range(s * CH, (s + 1) * CH):
            u[:, lanes(p)] = (row_scale(p) * x[0, :, lanes(p)]).astype(BF16)
        if s == STEPS - 1:
            mats[2].wait()
        products_down(s)
        start_p(0, s)
    mats[0].wait()
    mats[1].wait()
    for s in range(STEPS):
        local_step(s)

    def operation(k, last):
        par = lax.rem(k, 2)
        nxt = 1 - par
        fresh = lax.rem(k, DEGREE) == 0
        weight = jnp.where(fresh, 0.125, 0.25).astype(F32)
        for s in range(STEPS):
            wait_halo(par, s)
            for q in range(HALF + s * CH, HALF + (s + 1) * CH):
                value = recur(q, upper_total(par, q), par, weight, fresh)
                if last:
                    deal(q, value, f_out)
            for p in range(s * CH, (s + 1) * CH):
                value = recur(p, lower_total(par, p), par, weight, fresh)
                if last:
                    deal(p, value, f_out)
            products_down(s)
            start_u(nxt, s)
            start_p(nxt, s)
            if last:
                spread(f_out, f_all, fs_sem, fr_sem, s, F_WAYS)
                for r in runs_of(s):
                    out_copy(0, r).start()
                    out_copy(1, r).start()
            local_step(s)

    def loop_body(k, carry):
        operation(k, False)
        return carry

    lax.fori_loop(0, NOPS - 1, loop_body, 0)
    operation(NOPS - 1, True)

    for s in range(STEPS):
        wait_halo(NOPS % 2, s)
        for q in range(HALF + s * CH, HALF + (s + 1) * CH):
            deal(q, row_scale(q) * upper_total(NOPS % 2, q), g_out)
        for p in range(s * CH, (s + 1) * CH):
            deal(p, row_scale(p) * lower_total(NOPS % 2, p), g_out)
        spread(g_out, g_all, gs_sem, gr_sem, s, G_WAYS)

    for s in range(STEPS):
        for d in range(1, nv):
            exchange(f_out, f_all, fs_sem, fr_sem, s, d).wait_recv()
        part = dot(f_all[s], f_all[s], NT)
        q_buf[1] = part if s == 0 else q_buf[1] + part
    span = 128 // nv
    away = lax.rem(lax.broadcasted_iota(jnp.int32, (span, 128), 1) // span - v + nv, nv)
    q_buf[0] = jnp.zeros((128, 128), F32)
    own = jnp.zeros((span, span), F32)
    for s in range(STEPS):
        for j in range(nv):
            own = own + dot(g_out[s, j], f_out[s, j], NT)

    def group_rows(d):
        return pl.ds(pl.multiple_of(span * lax.rem(v + d, nv), span), span)

    for d, partners in ((0, (1, 2, 3)), (1, (2, 3)), (3, (2,))):
        part = jnp.zeros((span, 128), F32)
        for s in range(STEPS):
            if d > 0:
                exchange(g_out, g_all, gs_sem, gr_sem, s, nv - d).wait_recv()
            part = part + dot(g_all[s, group_rows(d), :], f_all[s], NT)
        keep = away == partners[0]
        for other in partners[1:]:
            keep = jnp.logical_or(keep, away == other)
        q_buf[0, group_rows(d), :] = jnp.where(keep, part, 0.0)
    q_buf[0] = q_buf[0] + q_buf[0].T
    q_buf[0, group_rows(0), :] += jnp.where(away == 0, jnp.concatenate([own] * nv, axis=1), 0.0)

    width = 128 // nm
    for i in range(nm):
        t_buf[i, 0:width, :] = q_buf[0, i * width : (i + 1) * width, :]
        t_buf[i, width : 2 * width, :] = q_buf[1, i * width : (i + 1) * width, :]

    def fold(d):
        to = lax.rem(m + d, nm)
        return pltpu.make_async_remote_copy(
            src_ref=t_buf.at[to],
            dst_ref=r_buf.at[d - 1],
            send_sem=ts_sem.at[d - 1],
            recv_sem=tr_sem.at[d - 1],
            device_id=(to, v),
            device_id_type=MESH,
        )

    def fold_start(d, carry):
        fold(d).start()
        return carry

    def fold_wait(d, carry):
        fold(d).wait_recv()
        return carry + r_buf[d - 1]

    lax.fori_loop(1, nm, fold_start, 0)
    s_buf[...] = lax.fori_loop(1, nm, fold_wait, t_buf[m])

    def fold_vec(d):
        return pltpu.make_async_remote_copy(
            src_ref=s_buf,
            dst_ref=r2_buf.at[d - 1],
            send_sem=s2_sem.at[d - 1],
            recv_sem=r2_sem.at[d - 1],
            device_id=(m, lax.rem(v + d, nv)),
            device_id_type=MESH,
        )

    for d in range(1, nv):
        fold_vec(d).start()
    total = s_buf[...]
    for d in range(1, nv):
        fold_vec(d).wait_recv()
        total = total + r2_buf[d - 1]
    cols = 128 // nv
    mine = jnp.zeros((2 * width, cols), F32)
    for j in range(nv):
        mine = jnp.where(v == j, total[:, j * cols : (j + 1) * cols], mine)
    ritz_ref[...] = mine

    for s in range(STEPS):
        for d in range(1, nv):
            exchange(f_out, f_all, fs_sem, fr_sem, s, d).wait_send()
        for d in G_WAYS:
            exchange(g_out, g_all, gs_sem, gr_sem, s, d).wait_send()

    def fold_left(d, carry):
        fold(d).wait_send()
        return carry

    lax.fori_loop(1, nm, fold_left, 0)
    for d in range(1, nv):
        fold_vec(d).wait_send()
    for h in range(2):
        for r in range(NRUN):
            out_copy(h, r).wait()


def write_out(filtered, ritz, out, stiff, massg, sem):
    copy = pltpu.make_async_copy(filtered, out, sem)
    copy.start()
    width = stiff.shape[0]
    stiff[...] = ritz[0:width]
    massg[...] = ritz[width : 2 * width]
    copy.wait()


def shards(nm, nv, panel, orient, mass, stiff_diag, near_coupling, far_coupling):
    rows, columns = panel.shape
    blocks = stiff_diag.shape[0]
    width = 128 // nm
    cols = 128 // nv
    anywhere = pl.BlockSpec(memory_space=pl.ANY)
    inside = pl.BlockSpec(memory_space=pltpu.VMEM)
    dma = pltpu.SemaphoreType.DMA
    mat = pltpu.VMEM((blocks, BS, BS), BF16)
    scratch = [
        pltpu.VMEM((blocks, BS), jnp.int32),
        pltpu.VMEM((blocks, BS), F32),
        pltpu.VMEM((blocks, BS), F32),
        mat, mat, mat,
        pltpu.VMEM((2, columns, rows), F32),
        pltpu.VMEM((columns, rows), F32),
        pltpu.VMEM((columns, rows), BF16),
        pltpu.VMEM((2, columns, HALF * BS), BF16),
        pltpu.VMEM((columns, (HALF + 1) * BS), BF16),
        pltpu.VMEM((2, columns, (HALF + 1) * BS), BF16),
        pltpu.VMEM((STEPS, nv, columns, rows // STEPS // nv), BF16),
        pltpu.VMEM((STEPS, nv, columns, rows // STEPS // nv), BF16),
        pltpu.VMEM((STEPS, nv * columns, rows // STEPS // nv), BF16),
        pltpu.VMEM((STEPS, nv * columns, rows // STEPS // nv), BF16),
        pltpu.VMEM((2, 128, 128), F32),
        pltpu.VMEM((nm, 2 * width, 128), F32),
        pltpu.VMEM((nm - 1, 2 * width, 128), F32),
        pltpu.VMEM((2 * width, 128), F32),
        pltpu.VMEM((nv - 1, 2 * width, 128), F32),
        dma((2,)), dma((2, NRUN)), dma((NRUN,)), dma((3,)), dma((2, NRUN)),
        dma((STEPS,)), dma((2, STEPS)), dma((STEPS,)), dma((2, STEPS)),
        dma((nv - 1, STEPS)), dma((nv - 1, STEPS)), dma((nv - 1, STEPS)), dma((nv - 1, STEPS)),
        dma((nm - 1,)), dma((nm - 1,)), dma((nv - 1,)), dma((nv - 1,)),
    ]
    filtered, ritz = pl.pallas_call(
        functools.partial(kernel, nm, nv),
        out_shape=(
            jax.ShapeDtypeStruct((columns, rows), F32),
            jax.ShapeDtypeStruct((2 * width, cols), F32),
        ),
        in_specs=[pl.BlockSpec(memory_space=pltpu.HBM)] * 6,
        out_specs=(anywhere, inside),
        scratch_shapes=scratch,
        compiler_params=pltpu.CompilerParams(
            collective_id=0, has_side_effects=True, vmem_limit_bytes=VMEM_LIMIT),
        name="filter_ritz",
    )(*[
        pltpu.with_memory_space_constraint(a, pltpu.HBM)
        for a in (
            panel.T,
            orient.reshape(blocks, BS),
            mass.reshape(blocks, BS),
            stiff_diag,
            near_coupling,
            far_coupling,
        )
    ])
    filtered, stiff, massg = pl.pallas_call(
        write_out,
        out_shape=(
            jax.ShapeDtypeStruct((columns, rows), F32),
            jax.ShapeDtypeStruct((width, cols), F32),
            jax.ShapeDtypeStruct((width, cols), F32),
        ),
        in_specs=[inside, inside],
        out_specs=(anywhere, inside, inside),
        scratch_shapes=[pltpu.SemaphoreType.DMA],
        compiler_params=pltpu.CompilerParams(vmem_limit_bytes=VMEM_LIMIT),
        name="write_out",
    )(filtered, ritz)
    return (filtered.T, stiff.T, massg.T)


def solution(mesh):
    placed = (
        P("mesh", "vec"),
        P("mesh"),
        P("mesh"),
        P("mesh", None, None),
        P("mesh", None, None),
        P("mesh", None, None),
    )
    return jax.shard_map(
        functools.partial(shards, mesh.shape["mesh"], mesh.shape["vec"]),
        mesh=mesh,
        in_specs=placed,
        out_specs=(P("mesh", "vec"), P("vec", "mesh"), P("vec", "mesh")),
        check_vma=False,
    )
```

```python
import functools

import jax
import jax.numpy as jnp
from jax import lax
from jax.experimental import pallas as pl
from jax.experimental.pallas import tpu as pltpu
from jax.sharding import PartitionSpec as P

SPAN = 32
BS = 128
DEGREE = 4
APPS = 2
NOPS = DEGREE * APPS
CENTER = 6.0

HALF = SPAN
STEPS = 4
CH = HALF // STEPS
GROUP = 8
F_WAYS = (2, 1, 3)
G_WAYS = (1, 3)
VMEM_LIMIT = 32 * 1024 * 1024

MESH = pl.DeviceIdType.MESH
NT = (((1,), (1,)), ((), ()))
NN = (((1,), (0,)), ((), ()))
F32 = jnp.float32
BF16 = jnp.bfloat16


def block_of(q):
    return HALF * (q // HALF) + (q % HALF + 1) % HALF


def place_of(b):
    return HALF * (b // HALF) + (b % HALF - 1) % HALF


def lanes(q, n=1):
    return slice(q * BS, (q + n) * BS)


def dot(a, b, dims):
    return lax.dot_general(a, b, dims, preferred_element_type=F32)


def pieces():
    runs = []
    for s in range(STEPS):
        count = CH if s < STEPS - 1 else CH - 1
        runs.append((s * CH, s * CH + 1, count))
    runs.append((HALF - 1, 0, 1))
    return runs


RUNS = pieces()
NRUN = len(RUNS)


def runs_of(s):
    return (s,) if s < STEPS - 1 else (s, s + 1)


def kernel(
    nm, nv,
    x_hbm, orient_hbm, mass_hbm, diag_hbm, near_hbm, far_hbm,
    out_hbm, ritz_ref,
    orient, mass, scale, diag, near, far,
    x, acc, u, halo_u, p_out, halo_p,
    f_out, g_out, f_all, g_all, q_buf, t_buf, r_buf, s_buf, r2_buf,
    vec_sem, x_sem, far_sem, mat_sem, o_sem,
    us_sem, ur_sem, ps_sem, pr_sem,
    fs_sem, fr_sem, gs_sem, gr_sem,
    ts_sem, tr_sem, s2_sem, r2_sem,
):
    m = lax.axis_index("mesh")
    v = lax.axis_index("vec")

    cp_or = pltpu.make_async_copy(orient_hbm, orient, vec_sem.at[0])
    cp_ma = pltpu.make_async_copy(mass_hbm, mass, vec_sem.at[1])
    cp_or.start()
    cp_ma.start()

    def x_copy(h, r):
        pos, blk, n = RUNS[r]
        return pltpu.make_async_copy(
            x_hbm.at[:, lanes(h * HALF + blk, n)],
            x.at[0, :, lanes(h * HALF + pos, n)],
            x_sem.at[h, r],
        )

    def far_copy(r):
        _, blk, n = RUNS[r]
        return pltpu.make_async_copy(far_hbm.at[pl.ds(blk, n)], far.at[pl.ds(blk, n)], far_sem.at[r])

    for r in range(NRUN):
        x_copy(0, r).start()
        x_copy(1, r).start()
        far_copy(r).start()

    mats = [
        pltpu.make_async_copy(far_hbm.at[pl.ds(HALF, HALF)], far.at[pl.ds(HALF, HALF)], mat_sem.at[0]),
        pltpu.make_async_copy(diag_hbm, diag, mat_sem.at[1]),
        pltpu.make_async_copy(near_hbm, near, mat_sem.at[2]),
    ]
    for c in mats:
        c.start()

    @pl.when(m == 0)
    def _():
        halo_u[...] = jnp.zeros_like(halo_u)

    @pl.when(m == nm - 1)
    def _():
        halo_p[...] = jnp.zeros_like(halo_p)

    barrier = pltpu.get_barrier_semaphore()

    group, member, ngroup = lax.div(m, GROUP), lax.rem(m, GROUP), nm // GROUP
    greeted = [(lax.rem(m + 1, nm), v), (lax.rem(m + nm - 1, nm), v)]
    greeted += [(lax.rem(group + d, ngroup) * GROUP + member, v) for d in range(1, ngroup)]
    greeted += [(m, lax.rem(v + d, nv)) for d in range(1, nv)]
    for peer in greeted:
        pl.semaphore_signal(barrier, inc=1, device_id=peer, device_id_type=MESH)

    cp_or.wait()
    cp_ma.wait()
    scale[...] = orient[...].astype(F32) / jnp.sqrt(mass[...])

    pl.semaphore_wait(barrier, len(greeted))

    def send_u(par, s):
        return pltpu.make_async_remote_copy(
            src_ref=u.at[:, lanes(HALF + s * CH, CH)],
            dst_ref=halo_u.at[par, :, lanes(s * CH, CH)],
            send_sem=us_sem.at[s],
            recv_sem=ur_sem.at[par, s],
            device_id=(m + 1, v),
            device_id_type=MESH,
        )

    def send_p(par, s):
        n = CH + (s == STEPS - 1)
        return pltpu.make_async_remote_copy(
            src_ref=p_out.at[:, lanes(s * CH, n)],
            dst_ref=halo_p.at[par, :, lanes(s * CH, n)],
            send_sem=ps_sem.at[s],
            recv_sem=pr_sem.at[par, s],
            device_id=(m - 1, v),
            device_id_type=MESH,
        )

    def start_u(par, s):
        @pl.when(m < nm - 1)
        def _():
            send_u(par, s).start()

    def start_p(par, s):
        @pl.when(m > 0)
        def _():
            send_p(par, s).start()

    def wait_halo(par, s, sends=True):
        @pl.when(m > 0)
        def _():
            send_u(par, s).wait_recv()
            send_p(par, s).wait_send()

        @pl.when(m < nm - 1)
        def _():
            send_p(par, s).wait_recv()
            send_u(par, s).wait_send()

    def row_scale(q):
        b = block_of(q)
        return scale[b : b + 1, :]

    def products_down(s):
        for p in range(s * CH, (s + 1) * CH):
            b = block_of(p)
            up = u[:, lanes(p)]
            p_out[:, lanes(p)] = dot(up, far[b], NN).astype(BF16)
            if b == 0:
                p_out[:, lanes(HALF)] = dot(up, near[0], NN).astype(BF16)

    def local_terms(q):
        b = block_of(q)
        at = lambda c: u[:, lanes(place_of(c))]
        if b < HALF:
            if b > 0:
                total = dot(
                    jnp.concatenate([at(b - 1), at(b)], axis=1),
                    jnp.concatenate([near[b], diag[b]], axis=1), NT)
            else:
                total = dot(at(b), diag[b], NT)
            total += dot(
                jnp.concatenate([at(b + 1), at(b + HALF)], axis=1),
                jnp.concatenate([near[b + 1], far[b + HALF]], axis=0), NN)
        else:
            total = dot(
                jnp.concatenate([at(b - 1), at(b - HALF)], axis=1),
                jnp.concatenate([near[b], far[b]], axis=1), NT)
            if b < 2 * HALF - 1:
                total += dot(
                    jnp.concatenate([at(b), at(b + 1)], axis=1),
                    jnp.concatenate([diag[b], near[b + 1]], axis=0), NN)
            else:
                total += dot(at(b), diag[b], NN)
        acc[:, lanes(q)] = total

    def local_places(s):
        if s == 0:
            places = range(1, CH - 1)
        elif s < STEPS - 1:
            places = range(s * CH - 1, (s + 1) * CH - 1)
        else:
            places = [*range(s * CH - 1, HALF), 0]
        return places

    def local_step(s):
        for p in local_places(s):
            local_terms(p)
            local_terms(HALF + p)

    def upper_total(par, q):
        p = q - HALF
        total = acc[:, lanes(q)] + halo_p[par, :, lanes(p)].astype(F32)
        if block_of(q) == 2 * HALF - 1:
            total += halo_p[par, :, lanes(HALF)].astype(F32)
        return total

    def lower_total(par, p):
        b = block_of(p)
        if b == 0:
            far_term = dot(
                jnp.concatenate([halo_u[par, :, lanes(p)], halo_u[par, :, lanes(p - 1)]], axis=1),
                jnp.concatenate([far[b], near[b]], axis=1), NT)
        else:
            far_term = dot(halo_u[par, :, lanes(p)], far[b], NT)
        return acc[:, lanes(p)] + far_term

    def recur(q, total, now, weight, fresh):
        image = row_scale(q) * total
        current = x[now, :, lanes(q)]
        before = x[1 - now, :, lanes(q)]
        following = weight * (image - CENTER * current) - jnp.where(fresh, 0.0, before)
        x[1 - now, :, lanes(q)] = following
        u[:, lanes(q)] = (row_scale(q) * following).astype(BF16)
        return following

    def deal(q, value, box):
        p = q % HALF
        s, r = p // CH, p % CH
        per = CH // nv
        box[s, r // per, :, lanes((q // HALF) * per + r % per)] = value.astype(BF16)

    def exchange(box, whole, ss, rs, s, d):
        to = lax.rem(v + d, nv)
        return pltpu.make_async_remote_copy(
            src_ref=box.at[s, to],
            dst_ref=whole.at[s, pl.ds(pl.multiple_of(32 * v, 32), 32), :],
            send_sem=ss.at[d - 1, s],
            recv_sem=rs.at[d - 1, s],
            device_id=(m, to),
            device_id_type=MESH,
        )

    def spread(box, whole, ss, rs, s, ways):
        for d in ways:
            exchange(box, whole, ss, rs, s, d).start()
        whole[s, pl.ds(pl.multiple_of(32 * v, 32), 32), :] = box[s, v]

    def out_copy(h, r):
        pos, blk, n = RUNS[r]
        return pltpu.make_async_copy(
            x.at[0, :, lanes(h * HALF + pos, n)],
            out_hbm.at[:, lanes(h * HALF + blk, n)],
            o_sem.at[h, r],
        )

    for s in range(STEPS):
        for r in runs_of(s):
            x_copy(1, r).wait()
        for q in range(HALF + s * CH, HALF + (s + 1) * CH):
            u[:, lanes(q)] = (row_scale(q) * x[0, :, lanes(q)]).astype(BF16)
        start_u(0, s)
        for r in runs_of(s):
            x_copy(0, r).wait()
            far_copy(r).wait()
        for p in range(s * CH, (s + 1) * CH):
            u[:, lanes(p)] = (row_scale(p) * x[0, :, lanes(p)]).astype(BF16)
        if s == STEPS - 1:
            mats[2].wait()
        products_down(s)
        start_p(0, s)
    mats[0].wait()
    mats[1].wait()
    for s in range(STEPS):
        local_step(s)

    def operation(k, last):
        par = lax.rem(k, 2)
        nxt = 1 - par
        fresh = lax.rem(k, DEGREE) == 0
        weight = jnp.where(fresh, 0.125, 0.25).astype(F32)
        for s in range(STEPS):
            wait_halo(par, s)
            for q in range(HALF + s * CH, HALF + (s + 1) * CH):
                value = recur(q, upper_total(par, q), par, weight, fresh)
                if last:
                    deal(q, value, f_out)
            for p in range(s * CH, (s + 1) * CH):
                value = recur(p, lower_total(par, p), par, weight, fresh)
                if last:
                    deal(p, value, f_out)
            products_down(s)
            start_u(nxt, s)
            start_p(nxt, s)
            if last:
                spread(f_out, f_all, fs_sem, fr_sem, s, F_WAYS)
                for r in runs_of(s):
                    out_copy(0, r).start()
                    out_copy(1, r).start()
            local_step(s)

    def loop_body(k, carry):
        operation(k, False)
        return carry

    lax.fori_loop(0, NOPS - 1, loop_body, 0)
    operation(NOPS - 1, True)

    for s in range(STEPS):
        wait_halo(NOPS % 2, s)
        for q in range(HALF + s * CH, HALF + (s + 1) * CH):
            deal(q, row_scale(q) * upper_total(NOPS % 2, q), g_out)
        for p in range(s * CH, (s + 1) * CH):
            deal(p, row_scale(p) * lower_total(NOPS % 2, p), g_out)
        spread(g_out, g_all, gs_sem, gr_sem, s, G_WAYS)

    for s in range(STEPS):
        for d in range(1, nv):
            exchange(f_out, f_all, fs_sem, fr_sem, s, d).wait_recv()
        part = dot(f_all[s], f_all[s], NT)
        q_buf[1] = part if s == 0 else q_buf[1] + part
    span = 128 // nv
    away = lax.rem(lax.broadcasted_iota(jnp.int32, (span, 128), 1) // span - v + nv, nv)
    q_buf[0] = jnp.zeros((128, 128), F32)
    own = jnp.zeros((span, span), F32)
    for s in range(STEPS):
        for j in range(nv):
            own = own + dot(g_out[s, j], f_out[s, j], NT)

    def group_rows(d):
        return pl.ds(pl.multiple_of(span * lax.rem(v + d, nv), span), span)

    for d, partners in ((0, (1, 2, 3)), (1, (2, 3)), (3, (2,))):
        part = jnp.zeros((span, 128), F32)
        for s in range(STEPS):
            if d > 0:
                exchange(g_out, g_all, gs_sem, gr_sem, s, nv - d).wait_recv()
            part = part + dot(g_all[s, group_rows(d), :], f_all[s], NT)
        keep = away == partners[0]
        for other in partners[1:]:
            keep = jnp.logical_or(keep, away == other)
        q_buf[0, group_rows(d), :] = jnp.where(keep, part, 0.0)
    q_buf[0] = q_buf[0] + q_buf[0].T
    q_buf[0, group_rows(0), :] += jnp.where(away == 0, jnp.concatenate([own] * nv, axis=1), 0.0)

    width = 128 // nm
    for i in range(nm):
        t_buf[i, 0:width, :] = q_buf[0, i * width : (i + 1) * width, :]
        t_buf[i, width : 2 * width, :] = q_buf[1, i * width : (i + 1) * width, :]

    def fold(d):
        to = lax.rem(m + d, nm)
        return pltpu.make_async_remote_copy(
            src_ref=t_buf.at[to],
            dst_ref=r_buf.at[d - 1],
            send_sem=ts_sem.at[d - 1],
            recv_sem=tr_sem.at[d - 1],
            device_id=(to, v),
            device_id_type=MESH,
        )

    def hops(d):
        chips = (d // GROUP, d % GROUP // 2)
        return sum(min(c, 4 - c) for c in chips)

    far_first = sorted(range(1, nm), key=hops, reverse=True)
    for d in far_first:
        fold(d).start()
    total = t_buf[m]
    for d in reversed(far_first):
        fold(d).wait_recv()
        total = total + r_buf[d - 1]
    s_buf[...] = total

    def fold_vec(d):
        return pltpu.make_async_remote_copy(
            src_ref=s_buf,
            dst_ref=r2_buf.at[d - 1],
            send_sem=s2_sem.at[d - 1],
            recv_sem=r2_sem.at[d - 1],
            device_id=(m, lax.rem(v + d, nv)),
            device_id_type=MESH,
        )

    for d in range(1, nv):
        fold_vec(d).start()
    total = s_buf[...]
    for d in range(1, nv):
        fold_vec(d).wait_recv()
        total = total + r2_buf[d - 1]
    cols = 128 // nv
    mine = jnp.zeros((2 * width, cols), F32)
    for j in range(nv):
        mine = jnp.where(v == j, total[:, j * cols : (j + 1) * cols], mine)
    ritz_ref[...] = mine

    for s in range(STEPS):
        for d in range(1, nv):
            exchange(f_out, f_all, fs_sem, fr_sem, s, d).wait_send()
        for d in G_WAYS:
            exchange(g_out, g_all, gs_sem, gr_sem, s, d).wait_send()

    def fold_left(d, carry):
        fold(d).wait_send()
        return carry

    lax.fori_loop(1, nm, fold_left, 0)
    for d in range(1, nv):
        fold_vec(d).wait_send()
    for h in range(2):
        for r in range(NRUN):
            out_copy(h, r).wait()


def write_out(filtered, ritz, out, stiff, massg, sem):
    copy = pltpu.make_async_copy(filtered, out, sem)
    copy.start()
    width = stiff.shape[0]
    stiff[...] = ritz[0:width]
    massg[...] = ritz[width : 2 * width]
    copy.wait()


def shards(nm, nv, panel, orient, mass, stiff_diag, near_coupling, far_coupling):
    rows, columns = panel.shape
    blocks = stiff_diag.shape[0]
    width = 128 // nm
    cols = 128 // nv
    anywhere = pl.BlockSpec(memory_space=pl.ANY)
    inside = pl.BlockSpec(memory_space=pltpu.VMEM)
    dma = pltpu.SemaphoreType.DMA
    mat = pltpu.VMEM((blocks, BS, BS), BF16)
    scratch = [
        pltpu.VMEM((blocks, BS), jnp.int32),
        pltpu.VMEM((blocks, BS), F32),
        pltpu.VMEM((blocks, BS), F32),
        mat, mat, mat,
        pltpu.VMEM((2, columns, rows), F32),
        pltpu.VMEM((columns, rows), F32),
        pltpu.VMEM((columns, rows), BF16),
        pltpu.VMEM((2, columns, HALF * BS), BF16),
        pltpu.VMEM((columns, (HALF + 1) * BS), BF16),
        pltpu.VMEM((2, columns, (HALF + 1) * BS), BF16),
        pltpu.VMEM((STEPS, nv, columns, rows // STEPS // nv), BF16),
        pltpu.VMEM((STEPS, nv, columns, rows // STEPS // nv), BF16),
        pltpu.VMEM((STEPS, nv * columns, rows // STEPS // nv), BF16),
        pltpu.VMEM((STEPS, nv * columns, rows // STEPS // nv), BF16),
        pltpu.VMEM((2, 128, 128), F32),
        pltpu.VMEM((nm, 2 * width, 128), F32),
        pltpu.VMEM((nm - 1, 2 * width, 128), F32),
        pltpu.VMEM((2 * width, 128), F32),
        pltpu.VMEM((nv - 1, 2 * width, 128), F32),
        dma((2,)), dma((2, NRUN)), dma((NRUN,)), dma((3,)), dma((2, NRUN)),
        dma((STEPS,)), dma((2, STEPS)), dma((STEPS,)), dma((2, STEPS)),
        dma((nv - 1, STEPS)), dma((nv - 1, STEPS)), dma((nv - 1, STEPS)), dma((nv - 1, STEPS)),
        dma((nm - 1,)), dma((nm - 1,)), dma((nv - 1,)), dma((nv - 1,)),
    ]
    filtered, ritz = pl.pallas_call(
        functools.partial(kernel, nm, nv),
        out_shape=(
            jax.ShapeDtypeStruct((columns, rows), F32),
            jax.ShapeDtypeStruct((2 * width, cols), F32),
        ),
        in_specs=[pl.BlockSpec(memory_space=pltpu.HBM)] * 6,
        out_specs=(anywhere, inside),
        scratch_shapes=scratch,
        compiler_params=pltpu.CompilerParams(
            collective_id=0, has_side_effects=True, vmem_limit_bytes=VMEM_LIMIT),
        name="filter_ritz",
    )(*[
        pltpu.with_memory_space_constraint(a, pltpu.HBM)
        for a in (
            panel.T,
            orient.reshape(blocks, BS),
            mass.reshape(blocks, BS),
            stiff_diag,
            near_coupling,
            far_coupling,
        )
    ])
    filtered, stiff, massg = pl.pallas_call(
        write_out,
        out_shape=(
            jax.ShapeDtypeStruct((columns, rows), F32),
            jax.ShapeDtypeStruct((width, cols), F32),
            jax.ShapeDtypeStruct((width, cols), F32),
        ),
        in_specs=[inside, inside],
        out_specs=(anywhere, inside, inside),
        scratch_shapes=[pltpu.SemaphoreType.DMA],
        compiler_params=pltpu.CompilerParams(vmem_limit_bytes=VMEM_LIMIT),
        name="write_out",
    )(filtered, ritz)
    return (filtered.T, stiff.T, massg.T)


def solution(mesh):
    placed = (
        P("mesh", "vec"),
        P("mesh"),
        P("mesh"),
        P("mesh", None, None),
        P("mesh", None, None),
        P("mesh", None, None),
    )
    return jax.shard_map(
        functools.partial(shards, mesh.shape["mesh"], mesh.shape["vec"]),
        mesh=mesh,
        in_specs=placed,
        out_specs=(P("mesh", "vec"), P("vec", "mesh"), P("vec", "mesh")),
        check_vma=False,
    )
```

```python
import functools

import jax
import jax.numpy as jnp
from jax import lax
from jax.experimental import pallas as pl
from jax.experimental.pallas import tpu as pltpu
from jax.sharding import PartitionSpec as P

SPAN = 32
BS = 128
DEGREE = 4
APPS = 2
NOPS = DEGREE * APPS
CENTER = 6.0

HALF = SPAN
STEPS = 8
CH = HALF // STEPS
GROUP = 8
F_WAYS = (2, 1, 3)
G_WAYS = (1, 3)
VMEM_LIMIT = 32 * 1024 * 1024

MESH = pl.DeviceIdType.MESH
NT = (((1,), (1,)), ((), ()))
NN = (((1,), (0,)), ((), ()))
F32 = jnp.float32
BF16 = jnp.bfloat16


def block_of(q):
    return HALF * (q // HALF) + (q % HALF + 1) % HALF


def place_of(b):
    return HALF * (b // HALF) + (b % HALF - 1) % HALF


def lanes(q, n=1):
    return slice(q * BS, (q + n) * BS)


def dot(a, b, dims):
    return lax.dot_general(a, b, dims, preferred_element_type=F32)


def pieces():
    runs = []
    for s in range(STEPS):
        count = CH if s < STEPS - 1 else CH - 1
        runs.append((s * CH, s * CH + 1, count))
    runs.append((HALF - 1, 0, 1))
    return runs


RUNS = pieces()
NRUN = len(RUNS)


def runs_of(s):
    return (s,) if s < STEPS - 1 else (s, s + 1)


def kernel(
    nm, nv,
    x_hbm, orient_hbm, mass_hbm, diag_hbm, near_hbm, far_hbm,
    out_hbm, ritz_ref,
    orient, mass, scale, diag, near, far,
    x, acc, u, halo_u, p_out, halo_p,
    f_out, g_out, f_all, g_all, q_buf, t_buf, r_buf, s_buf, r2_buf,
    vec_sem, x_sem, far_sem, mat_sem, o_sem,
    us_sem, ur_sem, ps_sem, pr_sem,
    fs_sem, fr_sem, gs_sem, gr_sem,
    ts_sem, tr_sem, s2_sem, r2_sem,
):
    m = lax.axis_index("mesh")
    v = lax.axis_index("vec")

    cp_or = pltpu.make_async_copy(orient_hbm, orient, vec_sem.at[0])
    cp_ma = pltpu.make_async_copy(mass_hbm, mass, vec_sem.at[1])
    cp_or.start()
    cp_ma.start()

    def x_copy(h, r):
        pos, blk, n = RUNS[r]
        return pltpu.make_async_copy(
            x_hbm.at[:, lanes(h * HALF + blk, n)],
            x.at[0, :, lanes(h * HALF + pos, n)],
            x_sem.at[h, r],
        )

    def far_copy(r):
        _, blk, n = RUNS[r]
        return pltpu.make_async_copy(far_hbm.at[pl.ds(blk, n)], far.at[pl.ds(blk, n)], far_sem.at[r])

    for r in range(NRUN):
        x_copy(0, r).start()
        x_copy(1, r).start()
        far_copy(r).start()

    mats = [
        pltpu.make_async_copy(far_hbm.at[pl.ds(HALF, HALF)], far.at[pl.ds(HALF, HALF)], mat_sem.at[0]),
        pltpu.make_async_copy(diag_hbm, diag, mat_sem.at[1]),
        pltpu.make_async_copy(near_hbm, near, mat_sem.at[2]),
    ]
    for c in mats:
        c.start()

    @pl.when(m == 0)
    def _():
        halo_u[...] = jnp.zeros_like(halo_u)

    @pl.when(m == nm - 1)
    def _():
        halo_p[...] = jnp.zeros_like(halo_p)

    barrier = pltpu.get_barrier_semaphore()

    group, member, ngroup = lax.div(m, GROUP), lax.rem(m, GROUP), nm // GROUP
    greeted = [(lax.rem(m + 1, nm), v), (lax.rem(m + nm - 1, nm), v)]
    greeted += [(lax.rem(group + d, ngroup) * GROUP + member, v) for d in range(1, ngroup)]
    greeted += [(m, lax.rem(v + d, nv)) for d in range(1, nv)]
    for peer in greeted:
        pl.semaphore_signal(barrier, inc=1, device_id=peer, device_id_type=MESH)

    cp_or.wait()
    cp_ma.wait()
    scale[...] = orient[...].astype(F32) / jnp.sqrt(mass[...])

    pl.semaphore_wait(barrier, len(greeted))

    def send_u(par, s):
        return pltpu.make_async_remote_copy(
            src_ref=u.at[:, lanes(HALF + s * CH, CH)],
            dst_ref=halo_u.at[par, :, lanes(s * CH, CH)],
            send_sem=us_sem.at[s],
            recv_sem=ur_sem.at[par, s],
            device_id=(m + 1, v),
            device_id_type=MESH,
        )

    def send_p(par, s):
        n = CH + (s == STEPS - 1)
        return pltpu.make_async_remote_copy(
            src_ref=p_out.at[:, lanes(s * CH, n)],
            dst_ref=halo_p.at[par, :, lanes(s * CH, n)],
            send_sem=ps_sem.at[s],
            recv_sem=pr_sem.at[par, s],
            device_id=(m - 1, v),
            device_id_type=MESH,
        )

    def start_u(par, s):
        @pl.when(m < nm - 1)
        def _():
            send_u(par, s).start()

    def start_p(par, s):
        @pl.when(m > 0)
        def _():
            send_p(par, s).start()

    def wait_halo(par, s, sends=True):
        @pl.when(m > 0)
        def _():
            send_u(par, s).wait_recv()
            send_p(par, s).wait_send()

        @pl.when(m < nm - 1)
        def _():
            send_p(par, s).wait_recv()
            send_u(par, s).wait_send()

    def row_scale(q):
        b = block_of(q)
        return scale[b : b + 1, :]

    def products_down(s):
        for p in range(s * CH, (s + 1) * CH):
            b = block_of(p)
            up = u[:, lanes(p)]
            p_out[:, lanes(p)] = dot(up, far[b], NN).astype(BF16)
            if b == 0:
                p_out[:, lanes(HALF)] = dot(up, near[0], NN).astype(BF16)

    def local_terms(q):
        b = block_of(q)
        at = lambda c: u[:, lanes(place_of(c))]
        if b < HALF:
            if b > 0:
                total = dot(
                    jnp.concatenate([at(b - 1), at(b)], axis=1),
                    jnp.concatenate([near[b], diag[b]], axis=1), NT)
            else:
                total = dot(at(b), diag[b], NT)
            total += dot(
                jnp.concatenate([at(b + 1), at(b + HALF)], axis=1),
                jnp.concatenate([near[b + 1], far[b + HALF]], axis=0), NN)
        else:
            total = dot(
                jnp.concatenate([at(b - 1), at(b - HALF)], axis=1),
                jnp.concatenate([near[b], far[b]], axis=1), NT)
            if b < 2 * HALF - 1:
                total += dot(
                    jnp.concatenate([at(b), at(b + 1)], axis=1),
                    jnp.concatenate([diag[b], near[b + 1]], axis=0), NN)
            else:
                total += dot(at(b), diag[b], NN)
        acc[:, lanes(q)] = total

    def local_places(s):
        if s == 0:
            places = range(1, CH - 1)
        elif s < STEPS - 1:
            places = range(s * CH - 1, (s + 1) * CH - 1)
        else:
            places = [*range(s * CH - 1, HALF), 0]
        return places

    def local_step(s):
        for p in local_places(s):
            local_terms(p)
            local_terms(HALF + p)

    def upper_total(par, q):
        p = q - HALF
        total = acc[:, lanes(q)] + halo_p[par, :, lanes(p)].astype(F32)
        if block_of(q) == 2 * HALF - 1:
            total += halo_p[par, :, lanes(HALF)].astype(F32)
        return total

    def lower_total(par, p):
        b = block_of(p)
        if b == 0:
            far_term = dot(
                jnp.concatenate([halo_u[par, :, lanes(p)], halo_u[par, :, lanes(p - 1)]], axis=1),
                jnp.concatenate([far[b], near[b]], axis=1), NT)
        else:
            far_term = dot(halo_u[par, :, lanes(p)], far[b], NT)
        return acc[:, lanes(p)] + far_term

    def recur(q, total, now, weight, fresh):
        image = row_scale(q) * total
        current = x[now, :, lanes(q)]
        before = x[1 - now, :, lanes(q)]
        following = weight * (image - CENTER * current) - jnp.where(fresh, 0.0, before)
        x[1 - now, :, lanes(q)] = following
        u[:, lanes(q)] = (row_scale(q) * following).astype(BF16)
        return following

    def deal(q, value, box):
        p = q % HALF
        s, r = p // CH, p % CH
        per = CH // nv
        box[s, r // per, :, lanes((q // HALF) * per + r % per)] = value.astype(BF16)

    def exchange(box, whole, ss, rs, s, d):
        to = lax.rem(v + d, nv)
        return pltpu.make_async_remote_copy(
            src_ref=box.at[s, to],
            dst_ref=whole.at[s, pl.ds(pl.multiple_of(32 * v, 32), 32), :],
            send_sem=ss.at[d - 1, s],
            recv_sem=rs.at[d - 1, s],
            device_id=(m, to),
            device_id_type=MESH,
        )

    def spread(box, whole, ss, rs, s, ways):
        for d in ways:
            exchange(box, whole, ss, rs, s, d).start()
        whole[s, pl.ds(pl.multiple_of(32 * v, 32), 32), :] = box[s, v]

    def out_copy(h, r):
        pos, blk, n = RUNS[r]
        return pltpu.make_async_copy(
            x.at[0, :, lanes(h * HALF + pos, n)],
            out_hbm.at[:, lanes(h * HALF + blk, n)],
            o_sem.at[h, r],
        )

    for s in range(STEPS):
        for r in runs_of(s):
            x_copy(1, r).wait()
        for q in range(HALF + s * CH, HALF + (s + 1) * CH):
            u[:, lanes(q)] = (row_scale(q) * x[0, :, lanes(q)]).astype(BF16)
        start_u(0, s)
        for r in runs_of(s):
            x_copy(0, r).wait()
            far_copy(r).wait()
        for p in range(s * CH, (s + 1) * CH):
            u[:, lanes(p)] = (row_scale(p) * x[0, :, lanes(p)]).astype(BF16)
        if s == STEPS - 1:
            mats[2].wait()
        products_down(s)
        start_p(0, s)
    mats[0].wait()
    mats[1].wait()
    for s in range(STEPS):
        local_step(s)

    def operation(k, last):
        par = lax.rem(k, 2)
        nxt = 1 - par
        fresh = lax.rem(k, DEGREE) == 0
        weight = jnp.where(fresh, 0.125, 0.25).astype(F32)
        for s in range(STEPS):
            wait_halo(par, s)
            for q in range(HALF + s * CH, HALF + (s + 1) * CH):
                value = recur(q, upper_total(par, q), par, weight, fresh)
                if last:
                    deal(q, value, f_out)
            for p in range(s * CH, (s + 1) * CH):
                value = recur(p, lower_total(par, p), par, weight, fresh)
                if last:
                    deal(p, value, f_out)
            if s > 0:
                local_step(s - 1)
            products_down(s)
            start_u(nxt, s)
            start_p(nxt, s)
            if last:
                spread(f_out, f_all, fs_sem, fr_sem, s, F_WAYS)
                for r in runs_of(s):
                    out_copy(0, r).start()
                    out_copy(1, r).start()
        local_step(STEPS - 1)

    def loop_body(k, carry):
        operation(k, False)
        return carry

    lax.fori_loop(0, NOPS - 1, loop_body, 0)
    operation(NOPS - 1, True)

    for s in range(STEPS):
        wait_halo(NOPS % 2, s)
        for q in range(HALF + s * CH, HALF + (s + 1) * CH):
            deal(q, row_scale(q) * upper_total(NOPS % 2, q), g_out)
        for p in range(s * CH, (s + 1) * CH):
            deal(p, row_scale(p) * lower_total(NOPS % 2, p), g_out)
        spread(g_out, g_all, gs_sem, gr_sem, s, G_WAYS)

    for s in range(STEPS):
        for d in range(1, nv):
            exchange(f_out, f_all, fs_sem, fr_sem, s, d).wait_recv()
        part = dot(f_all[s], f_all[s], NT)
        q_buf[1] = part if s == 0 else q_buf[1] + part
    span = 128 // nv
    away = lax.rem(lax.broadcasted_iota(jnp.int32, (span, 128), 1) // span - v + nv, nv)
    q_buf[0] = jnp.zeros((128, 128), F32)
    own = jnp.zeros((span, span), F32)
    for s in range(STEPS):
        for j in range(nv):
            own = own + dot(g_out[s, j], f_out[s, j], NT)

    def group_rows(d):
        return pl.ds(pl.multiple_of(span * lax.rem(v + d, nv), span), span)

    for d, partners in ((0, (1, 2, 3)), (1, (2, 3)), (3, (2,))):
        part = jnp.zeros((span, 128), F32)
        for s in range(STEPS):
            if d > 0:
                exchange(g_out, g_all, gs_sem, gr_sem, s, nv - d).wait_recv()
            part = part + dot(g_all[s, group_rows(d), :], f_all[s], NT)
        keep = away == partners[0]
        for other in partners[1:]:
            keep = jnp.logical_or(keep, away == other)
        q_buf[0, group_rows(d), :] = jnp.where(keep, part, 0.0)
    q_buf[0] = q_buf[0] + q_buf[0].T
    q_buf[0, group_rows(0), :] += jnp.where(away == 0, jnp.concatenate([own] * nv, axis=1), 0.0)

    width = 128 // nm
    for i in range(nm):
        t_buf[i, 0:width, :] = q_buf[0, i * width : (i + 1) * width, :]
        t_buf[i, width : 2 * width, :] = q_buf[1, i * width : (i + 1) * width, :]

    def fold(d):
        to = lax.rem(m + d, nm)
        return pltpu.make_async_remote_copy(
            src_ref=t_buf.at[to],
            dst_ref=r_buf.at[d - 1],
            send_sem=ts_sem.at[d - 1],
            recv_sem=tr_sem.at[d - 1],
            device_id=(to, v),
            device_id_type=MESH,
        )

    def hops(d):
        chips = (d // GROUP, d % GROUP // 2)
        return sum(min(c, 4 - c) for c in chips)

    far_first = sorted(range(1, nm), key=hops, reverse=True)
    for d in far_first:
        fold(d).start()
    total = t_buf[m]
    for d in reversed(far_first):
        fold(d).wait_recv()
        total = total + r_buf[d - 1]
    s_buf[...] = total

    def fold_vec(d):
        return pltpu.make_async_remote_copy(
            src_ref=s_buf,
            dst_ref=r2_buf.at[d - 1],
            send_sem=s2_sem.at[d - 1],
            recv_sem=r2_sem.at[d - 1],
            device_id=(m, lax.rem(v + d, nv)),
            device_id_type=MESH,
        )

    for d in range(1, nv):
        fold_vec(d).start()
    total = s_buf[...]
    for d in range(1, nv):
        fold_vec(d).wait_recv()
        total = total + r2_buf[d - 1]
    cols = 128 // nv
    mine = jnp.zeros((2 * width, cols), F32)
    for j in range(nv):
        mine = jnp.where(v == j, total[:, j * cols : (j + 1) * cols], mine)
    ritz_ref[...] = mine

    for s in range(STEPS):
        for d in range(1, nv):
            exchange(f_out, f_all, fs_sem, fr_sem, s, d).wait_send()
        for d in G_WAYS:
            exchange(g_out, g_all, gs_sem, gr_sem, s, d).wait_send()

    def fold_left(d, carry):
        fold(d).wait_send()
        return carry

    lax.fori_loop(1, nm, fold_left, 0)
    for d in range(1, nv):
        fold_vec(d).wait_send()
    for h in range(2):
        for r in range(NRUN):
            out_copy(h, r).wait()


def write_out(filtered, ritz, out, stiff, massg, sem):
    copy = pltpu.make_async_copy(filtered, out, sem)
    copy.start()
    width = stiff.shape[0]
    stiff[...] = ritz[0:width]
    massg[...] = ritz[width : 2 * width]
    copy.wait()


def shards(nm, nv, panel, orient, mass, stiff_diag, near_coupling, far_coupling):
    rows, columns = panel.shape
    blocks = stiff_diag.shape[0]
    width = 128 // nm
    cols = 128 // nv
    anywhere = pl.BlockSpec(memory_space=pl.ANY)
    inside = pl.BlockSpec(memory_space=pltpu.VMEM)
    dma = pltpu.SemaphoreType.DMA
    mat = pltpu.VMEM((blocks, BS, BS), BF16)
    scratch = [
        pltpu.VMEM((blocks, BS), jnp.int32),
        pltpu.VMEM((blocks, BS), F32),
        pltpu.VMEM((blocks, BS), F32),
        mat, mat, mat,
        pltpu.VMEM((2, columns, rows), F32),
        pltpu.VMEM((columns, rows), F32),
        pltpu.VMEM((columns, rows), BF16),
        pltpu.VMEM((2, columns, HALF * BS), BF16),
        pltpu.VMEM((columns, (HALF + 1) * BS), BF16),
        pltpu.VMEM((2, columns, (HALF + 1) * BS), BF16),
        pltpu.VMEM((STEPS, nv, columns, rows // STEPS // nv), BF16),
        pltpu.VMEM((STEPS, nv, columns, rows // STEPS // nv), BF16),
        pltpu.VMEM((STEPS, nv * columns, rows // STEPS // nv), BF16),
        pltpu.VMEM((STEPS, nv * columns, rows // STEPS // nv), BF16),
        pltpu.VMEM((2, 128, 128), F32),
        pltpu.VMEM((nm, 2 * width, 128), F32),
        pltpu.VMEM((nm - 1, 2 * width, 128), F32),
        pltpu.VMEM((2 * width, 128), F32),
        pltpu.VMEM((nv - 1, 2 * width, 128), F32),
        dma((2,)), dma((2, NRUN)), dma((NRUN,)), dma((3,)), dma((2, NRUN)),
        dma((STEPS,)), dma((2, STEPS)), dma((STEPS,)), dma((2, STEPS)),
        dma((nv - 1, STEPS)), dma((nv - 1, STEPS)), dma((nv - 1, STEPS)), dma((nv - 1, STEPS)),
        dma((nm - 1,)), dma((nm - 1,)), dma((nv - 1,)), dma((nv - 1,)),
    ]
    filtered, ritz = pl.pallas_call(
        functools.partial(kernel, nm, nv),
        out_shape=(
            jax.ShapeDtypeStruct((columns, rows), F32),
            jax.ShapeDtypeStruct((2 * width, cols), F32),
        ),
        in_specs=[pl.BlockSpec(memory_space=pltpu.HBM)] * 6,
        out_specs=(anywhere, inside),
        scratch_shapes=scratch,
        compiler_params=pltpu.CompilerParams(
            collective_id=0, has_side_effects=True, vmem_limit_bytes=VMEM_LIMIT),
        name="filter_ritz",
    )(*[
        pltpu.with_memory_space_constraint(a, pltpu.HBM)
        for a in (
            panel.T,
            orient.reshape(blocks, BS),
            mass.reshape(blocks, BS),
            stiff_diag,
            near_coupling,
            far_coupling,
        )
    ])
    filtered, stiff, massg = pl.pallas_call(
        write_out,
        out_shape=(
            jax.ShapeDtypeStruct((columns, rows), F32),
            jax.ShapeDtypeStruct((width, cols), F32),
            jax.ShapeDtypeStruct((width, cols), F32),
        ),
        in_specs=[inside, inside],
        out_specs=(anywhere, inside, inside),
        scratch_shapes=[pltpu.SemaphoreType.DMA],
        compiler_params=pltpu.CompilerParams(vmem_limit_bytes=VMEM_LIMIT),
        name="write_out",
    )(filtered, ritz)
    return (filtered.T, stiff.T, massg.T)


def solution(mesh):
    placed = (
        P("mesh", "vec"),
        P("mesh"),
        P("mesh"),
        P("mesh", None, None),
        P("mesh", None, None),
        P("mesh", None, None),
    )
    return jax.shard_map(
        functools.partial(shards, mesh.shape["mesh"], mesh.shape["vec"]),
        mesh=mesh,
        in_specs=placed,
        out_specs=(P("mesh", "vec"), P("vec", "mesh"), P("vec", "mesh")),
        check_vma=False,
    )
```
